256 devices in a mesh: lat: 4 (over x_lo, core), wide: 64 (over x_hi, z, y).
Axes of the slice: x: 4 (x_hi: 2, x_lo: 2; x = x_hi * 2 + x_lo), y: 4, z: 8, core: 2. Of those that a mesh axis runs over, the one named last changes fastest.
Arguments:
- fields: float32 [4, 128, 128, 256], P(None, 'wide', 'lat'), may hold values from -4 to 4
- w_first: bfloat16 [3, 4, 64], replicated, may hold values from -1.75 to 1.75
- w_second: bfloat16 [3, 64, 64], replicated, may hold values from -0.4375 to 0.4375
- w_third: bfloat16 [3, 64, 64], replicated, may hold values from -0.4375 to 0.4375
- w_last: bfloat16 [3, 64, 4], replicated, may hold values from -0.4375 to 0.4375
Outputs:
- stepped: float32 [4, 128, 128, 256], P(None, 'wide', 'lat')
The draws below stay inside these ranges and needn't reach their ends.
All inputs are finite; a program needn't handle non-finite values.
Results may differ from the reference program's by a relative error of at most 0.0056.
Values may be sent and summed in bfloat16 or wider, within the bound.
A program may use at most 64 MiB of HBM per device.

```python
import jax
import jax.numpy as jnp
from jax import lax

NLON = 256
CHAN = 64
FIELDS = 4
NLAT = 128
NLEV = 128


def steps_of(key, extent, split, least, largest):
    factor_of = 1.0
    for axis_at, blocks in split:
        steps = jax.random.uniform(jax.random.fold_in(jax.random.fold_in(key, 6), axis_at), (blocks,), jnp.float32, least / len(split), largest / len(split))
        factor_of = factor_of * jnp.repeat(jnp.exp(steps), extent[axis_at] // blocks).reshape((-1,) + (1,) * (len(extent) - 1 - axis_at))
    return factor_of


def noise(key, dims, width, reach, shards=(), held_as=jnp.bfloat16):
    array = jax.random.normal(key, dims, jnp.float32) * width
    if len(shards) > 0:
        array = steps_of(key, dims, shards, -0.22, 0.18) * array
    return jnp.clip(array, min=-reach, max=reach).astype(held_as)


def setup_inputs(seed: int = 0) -> dict:
    seeds = jax.random.split(jax.random.key(seed), 6)
    fields = noise(seeds[0], (FIELDS, NLEV, NLAT, NLON), 1.0, 4.0, ((1, 64), (2, 4)), jnp.float32)
    w_first = noise(seeds[1], (3, FIELDS, CHAN), (3 * FIELDS) ** -0.5, 1.75)
    w_second = noise(seeds[2], (3, CHAN, CHAN), (3 * CHAN) ** -0.5, 0.4375)
    w_third = noise(seeds[3], (3, CHAN, CHAN), (3 * CHAN) ** -0.5, 0.4375)
    w_last = noise(seeds[4], (3, CHAN, FIELDS), (3 * CHAN) ** -0.5, 0.4375)
    return {"fields": fields, "w_first": w_first, "w_second": w_second, "w_third": w_third, "w_last": w_last}


courant = 0.3
smooth_eps = 0.01

def smooth_abs(values):
    return jnp.sqrt(values * values + smooth_eps)

def advect(extended, at_south, at_north):
    cells = extended[:, :, 1:-1, :]
    east_wind = cells[0]
    east_face = 0.5 * (east_wind + jnp.roll(east_wind, -1, axis=2))
    neighbour = jnp.roll(cells, -1, axis=3)
    east_flux = 0.5 * east_face * (cells + neighbour) - 0.5 * smooth_abs(east_face) * (neighbour - cells)
    east_div = east_flux - jnp.roll(east_flux, 1, axis=3)
    north_wind = extended[1]
    north_face = 0.5 * (north_wind[:, :-1] + north_wind[:, 1:])
    below_rows = extended[:, :, :-1]
    above_rows = extended[:, :, 1:]
    north_flux = 0.5 * north_face * (below_rows + above_rows) - 0.5 * smooth_abs(north_face) * (above_rows - below_rows)
    n_faces = north_flux.shape[2]
    row_index = lax.broadcasted_iota(jnp.int32, (1, 1, n_faces, 1), 2)
    closed = jnp.logical_or(jnp.logical_and(row_index == 0, at_south), jnp.logical_and(row_index == n_faces - 1, at_north))
    north_flux = jnp.where(closed, jnp.float32(0.0), north_flux)
    north_div = north_flux[:, :, 1:] - north_flux[:, :, :-1]
    return cells - courant * (east_div + north_div)

def conv_levels(inputs, kernel):
    padded = jnp.pad(inputs.astype(jnp.float32), ((0, 0), (0, 0), (1, 1)))
    n_lev = inputs.shape[2]
    result = jnp.zeros((kernel.shape[2], inputs.shape[1], n_lev), jnp.float32)
    for tap in range(3):
        result = result + jnp.einsum('cbl,co->obl', padded[:, :, tap:tap + n_lev], kernel[tap].astype(jnp.float32))
    return result

def column_net(inputs, w_first, w_second, w_third, w_last):
    hidden = jax.nn.silu(conv_levels(inputs, w_first)).astype(jnp.bfloat16)
    hidden = (hidden.astype(jnp.float32) + jax.nn.silu(conv_levels(hidden, w_second))).astype(jnp.bfloat16)
    hidden = (hidden.astype(jnp.float32) + jax.nn.silu(conv_levels(hidden, w_third))).astype(jnp.bfloat16)
    return conv_levels(hidden, w_last)

def reference(fields, w_first, w_second, w_third, w_last):
    padded = jnp.pad(fields, ((0, 0), (0, 0), (1, 1), (0, 0)))
    advected = advect(padded, True, True)
    inputs = advected.astype(jnp.bfloat16)

    def one_band(band_row):
        column = jnp.transpose(band_row, (0, 2, 1))
        result = column_net(column, w_first, w_second, w_third, w_last)
        return jnp.transpose(result, (0, 2, 1))
    tendency = lax.map(one_band, jnp.transpose(inputs, (2, 0, 1, 3)))
    tendency = jnp.transpose(tendency, (1, 2, 0, 3))
    updated = advected + tendency
    padded_two = jnp.pad(updated, ((0, 0), (0, 0), (1, 1), (0, 0)))
    return advect(padded_two, True, True)
```

```python
import jax
import jax.numpy as jnp
from jax import lax
from jax.experimental import pallas as pl
from jax.experimental.pallas import tpu as pltpu
from jax.sharding import PartitionSpec as P

MESH = pl.DeviceIdType.MESH
F32 = jnp.float32
BF16 = jnp.bfloat16

G = 4
R = 9
STARTS = (0, 8, 17, 25)
CH = 3
NCH = R // CH
SLABS = G + 4


def smooth_abs(v):
    return jnp.sqrt(v * v + 0.01)


def spread(v, first):
    sub = lax.broadcasted_iota(jnp.int32, v.shape, 0)
    if first == 0:
        pair = jnp.where(sub < 2, v, pltpu.roll(v, 2, 0))
    else:
        pair = jnp.where(sub < 2, pltpu.roll(v, 6, 0), v)
    return jnp.where(sub < 4, pair, pltpu.roll(pair, 4, 0))


def transport(rows, masks):
    n = len(rows) - 2
    winds = [spread(v, 2) for v in rows]
    fluxes = []
    for j in range(n + 1):
        low, high = rows[j], rows[j + 1]
        face = 0.5 * (winds[j] + winds[j + 1])
        flux = 0.5 * face * (low + high) - 0.5 * smooth_abs(face) * (high - low)
        if j in masks:
            flux = flux * masks[j]
        fluxes.append(flux)
    outs = []
    for j in range(n):
        cell = rows[j + 1]
        lanes = cell.shape[1]
        wind = spread(cell, 0)
        face = 0.5 * (wind + pltpu.roll(wind, lanes - 1, 1))
        after = pltpu.roll(cell, lanes - 1, 1)
        flux = 0.5 * face * (cell + after) - 0.5 * smooth_abs(face) * (after - cell)
        div = flux - pltpu.roll(flux, 1, 1)
        outs.append(cell - 0.3 * (div + (fluxes[j + 1] - fluxes[j])))
    return outs


def act(t):
    return t + t * jnp.tanh(t)


def dot(a, b):
    return jnp.dot(a, b, preferred_element_type=F32)


def kernel(
    f_hbm, w1_ref, w2_ref, w3_ref, w4_ref, out_ref,
    ext, adv, packed, xbuf, tsend, tin, outv, wa, wb2, wb3, wd, stage, h1, h2, h3,
    in_sem, halo_send, halo_recv, x_send, x_recv, t_send, t_recv,
):
    lat = lax.axis_index("lat")
    wide = lax.axis_index("wide")
    n_lat = lax.axis_size("lat")
    n_groups = lax.axis_size("wide") // G
    grp = wide // G
    m = wide % G
    at_south = lat == 0
    at_north = lat == n_lat - 1
    up = m >= 2
    og = jnp.where(up, grp + 1, grp - 1)
    os = jnp.where(up, m - 2, m + G + 2)
    has_other = jnp.logical_and(og >= 0, og < n_groups)

    barrier = pltpu.get_barrier_semaphore()

    def greet(la, wi):
        pl.semaphore_signal(barrier, inc=1, device_id=(la, wi), device_id_type=MESH)

    @pl.when(grp > 0)
    def _():
        for k in (2, 3):
            greet(lat, (grp - 1) * G + k)

    @pl.when(grp < n_groups - 1)
    def _():
        for k in (0, 1):
            greet(lat, (grp + 1) * G + k)

    for k in range(G):
        @pl.when(m != k)
        def _():
            greet(lat, grp * G + k)

    @pl.when(jnp.logical_not(at_south))
    def _():
        greet(lat - 1, wide)

    @pl.when(jnp.logical_not(at_north))
    def _():
        greet(lat + 1, wide)

    loads = []
    for f in range(4):
        for l in range(2):
            loads.append(
                pltpu.make_async_copy(
                    f_hbm.at[f, l], ext.at[pl.ds(2, 32), 2 * f + l], in_sem.at[2 * f + l]
                )
            )
    for c in loads:
        c.start()

    @pl.when(at_south)
    def _():
        ext[0:2] = jnp.zeros((2, 8, 256), F32)

    @pl.when(at_north)
    def _():
        ext[34:36] = jnp.zeros((2, 8, 256), F32)

    @pl.when(grp == 0)
    def _():
        xbuf[0:2] = jnp.zeros((2, R, 8, 256), BF16)

    @pl.when(grp == n_groups - 1)
    def _():
        xbuf[G + 2 : G + 4] = jnp.zeros((2, R, 8, 256), BF16)

    for c in loads:
        c.wait()

    def first_body(c, carry):
        e = 2 + 5 * c
        outs = transport([ext[e + i] for i in range(7)], {})
        for i in range(5):
            adv[e + i] = outs[i]
            packed[e + i] = outs[i].astype(BF16)
        return carry

    lax.fori_loop(0, 6, first_body, 0)

    expected = (
        (G - 1)
        + jnp.where(at_south, 0, 1)
        + jnp.where(at_north, 0, 1)
        + jnp.where(has_other, G, 0)
    )
    pl.semaphore_wait(barrier, expected)

    to_north = pltpu.make_async_remote_copy(
        ext.at[pl.ds(32, 2)], ext.at[pl.ds(0, 2)], halo_send.at[0], halo_recv.at[0],
        device_id=(lat + 1, wide), device_id_type=MESH,
    )
    to_south = pltpu.make_async_remote_copy(
        ext.at[pl.ds(2, 2)], ext.at[pl.ds(34, 2)], halo_send.at[1], halo_recv.at[1],
        device_id=(lat - 1, wide), device_id_type=MESH,
    )

    @pl.when(jnp.logical_not(at_north))
    def _():
        to_north.start()

    @pl.when(jnp.logical_not(at_south))
    def _():
        to_south.start()

    def local_row(k, c):
        return (NCH - 1 - c) * CH if k == 0 else c * CH

    def x_copy(k, c, group, slab, sem):
        row = local_row(k, c)
        return pltpu.make_async_remote_copy(
            packed.at[pl.ds(STARTS[k] + row, CH)],
            xbuf.at[slab, pl.ds(row, CH)],
            x_send.at[sem, k, c],
            x_recv.at[slab, c],
            device_id=(lat, group * G + k),
            device_id_type=MESH,
        )

    def each_x(k, c, act_on):
        @pl.when(has_other)
        def _():
            act_on(x_copy(k, c, og, os, 1))

        @pl.when(m != k)
        def _():
            act_on(x_copy(k, c, grp, m + 2, 0))

    for c in range(NCH):
        for k in range(G):
            if c < NCH - 1 or k in (1, 2):
                each_x(k, c, lambda d: d.start())

    @pl.when(jnp.logical_not(at_south))
    def _():
        to_north.wait_recv()

    @pl.when(jnp.logical_not(at_north))
    def _():
        to_south.wait_recv()

    south_open = jnp.where(at_south, 0.0, 1.0).astype(F32)
    north_open = jnp.where(at_north, 0.0, 1.0).astype(F32)
    for e, mask in ((0, south_open), (32, north_open)):
        outs = transport([ext[e + i] for i in range(4)], {1: mask})
        for i in range(2):
            adv[e + i] = outs[i]
            packed[e + i] = outs[i].astype(BF16)
    for k in (0, 3):
        each_x(k, NCH - 1, lambda d: d.start())

    mine = (25 * m + 1) // 3
    xbuf[pl.ds(m + 2, 1)] = packed[pl.ds(mine, R)][None]

    def iota(shape, d):
        return lax.broadcasted_iota(jnp.int32, shape, d)

    def one(cond):
        return jnp.where(cond, 1.0, 0.0)

    eye = one(iota((64, 64), 0) == iota((64, 64), 1)).astype(BF16)

    def transposed(w):
        return lax.dot_general(eye, w, (((1,), (1,)), ((), ())), preferred_element_type=F32)

    stage[...] = jnp.zeros((24, 64), F32)
    for k in range(3):
        stage[8 * k : 8 * k + 4] = w1_ref[k].astype(F32)
    w1t = (0.5 * transposed(stage[...].astype(BF16))).astype(BF16)
    row = iota((24, 64), 0)
    col = iota((24, 64), 1)
    same_field = (row & 7) == ((col & 7) >> 1)
    level_in = 2 * (col >> 3) + (col & 1)
    for j in range(14):
        band = one(jnp.logical_and(same_field, level_in == j + (row >> 3))).astype(BF16)
        level = 2 * G * grp + j - 3
        valid = jnp.where(
            jnp.logical_and(level >= 0, level < 2 * G * n_groups), 1.0, 0.0
        ).astype(F32)
        wa[64 * j : 64 * j + 64] = (dot(w1t, band) * valid).astype(BF16)
    zeros = jnp.zeros((64, 64), F32)
    for w_ref, band_ref in ((w2_ref, wb2), (w3_ref, wb3)):
        taps = [0.5 * transposed(w_ref[k]) for k in range(3)]
        for o in range(6):
            off = o - 2
            parts = [taps[i - off] if 0 <= i - off < 3 else zeros for i in range(4)]
            band_ref[64 * o : 64 * o + 64] = jnp.concatenate(parts, axis=1).astype(BF16)
    rho = iota((32, 64), 0)
    level_out = 2 * (rho >> 3) + (rho & 1)
    stage[0:8] = jnp.zeros((8, 64), F32)
    pick = one(iota((32, 8), 1) == ((iota((32, 8), 0) & 7) >> 1)).astype(BF16)
    last = []
    for k in range(3):
        stage[0:4] = w4_ref[k].astype(F32)
        last.append(dot(pick, stage[0:8].astype(BF16)))
    for t in range(3):
        parts = []
        for i in range(4):
            part = jnp.zeros((32, 64), F32)
            for k in range(3):
                part = part + jnp.where(level_out == 4 * t + i - k, last[k], 0.0)
            parts.append(part)
        wd[t] = jnp.concatenate(parts, axis=1).astype(BF16)

    low_valid = jnp.where(grp == 0, 0.0, 1.0).astype(F32)
    high_valid = jnp.where(grp == n_groups - 1, 0.0, 1.0).astype(F32)

    def one_row(r):
        x = jnp.concatenate([xbuf[s, r].astype(F32) for s in range(SLABS)], axis=0).astype(BF16)
        for q in range(7):
            h1[128 * q : 128 * q + 128] = act(dot(wa[128 * q : 128 * q + 128], x)).astype(BF16)
        y0 = dot(wb2[128:384], h1[0:256])
        y1 = dot(wb2[...], h1[256:512])
        y2 = dot(wb2[...], h1[512:768])
        y3 = dot(wb2[0:128, 0:128], h1[768:896])
        z = (
            y0[0:128] * low_valid, y0[128:256] + y1[0:128], y1[128:256],
            y1[256:384] + y2[0:128], y2[128:256], (y2[256:384] + y3) * high_valid,
        )
        for p in range(6):
            held = h1[64 + 128 * p : 192 + 128 * p].astype(F32)
            h2[128 * p : 128 * p + 128] = (held + act(z[p])).astype(BF16)
        y0 = dot(wb3[128:384], h2[0:256])
        y1 = dot(wb3[...], h2[256:512])
        y2 = dot(wb3[0:256], h2[512:768])
        z = (
            y0[0:64] * low_valid, y0[64:128], y0[128:256] + y1[0:128], y1[128:256],
            y1[256:384] + y2[0:128], y2[128:192], y2[192:256] * high_valid,
        )
        at = 0
        for v in z:
            size = v.shape[0]
            held = h2[64 + at : 64 + at + size].astype(F32)
            h3[at : at + size] = (held + act(v)).astype(BF16)
            at += size
        out = dot(wd[0], h3[0:256]) + dot(wd[1], h3[256:512]) + dot(wd[2][:, 0:128], h3[512:640])
        for k in range(G):
            tsend[k, r] = out[8 * k : 8 * k + 8].astype(BF16)

    def base_of(c):
        return jnp.where(m == 0, (NCH - 1 - c) * CH, c * CH)

    def t_copy(k, c):
        return pltpu.make_async_remote_copy(
            tsend.at[k, pl.ds(base_of(c), CH)],
            tin.at[m, pl.ds(base_of(c), CH)],
            t_send.at[k, c],
            t_recv.at[m, c],
            device_id=(lat, grp * G + k),
            device_id_type=MESH,
        )

    def x_arrived(s, c):
        d = pltpu.make_async_remote_copy(
            packed.at[pl.ds(0, CH)], xbuf.at[s, pl.ds(base_of(c), CH)],
            x_send.at[0, 0, c], x_recv.at[s, c], device_id=(lat, wide), device_id_type=MESH,
        )
        d.wait_recv()

    for c in range(NCH):
        for s in range(SLABS):
            if s < 2:
                cond = grp > 0
            elif s >= G + 2:
                cond = grp < n_groups - 1
            else:
                cond = m != s - 2

            @pl.when(cond)
            def _():
                x_arrived(s, c)

        def row_body(i, carry):
            one_row(base_of(c) + i)
            return carry

        lax.fori_loop(0, CH, row_body, 0)
        for k in range(G):
            @pl.when(m != k)
            def _():
                t_copy(k, c).start()

    tin[pl.ds(m, 1)] = tsend[pl.ds(m, 1)]

    for k in range(G):
        @pl.when(m != k)
        def _():
            for c in range(NCH):
                d = pltpu.make_async_remote_copy(
                    tsend.at[k, pl.ds(local_row(k, c), CH)],
                    tin.at[k, pl.ds(local_row(k, c), CH)],
                    t_send.at[k, c], t_recv.at[k, c],
                    device_id=(lat, wide), device_id_type=MESH,
                )
                d.wait_recv()

        first = STARTS[k] if k == 0 else STARTS[k - 1] + R
        for e in range(first, STARTS[k] + R):
            adv[e] = adv[e] + tin[k, e - STARTS[k]].astype(F32)

    def second_body(c, carry):
        e = 4 * c
        low = jnp.where(jnp.logical_and(at_south, c == 0), 0.0, 1.0).astype(F32)
        high = jnp.where(jnp.logical_and(at_north, c == 7), 0.0, 1.0).astype(F32)
        outs = transport([adv[e + i] for i in range(6)], {0: low, 4: high})
        for i in range(4):
            outv[e + i] = outs[i]
        return carry

    lax.fori_loop(0, 8, second_body, 0)
    stores = []
    for f in range(4):
        for l in range(2):
            stores.append(
                pltpu.make_async_copy(
                    outv.at[:, 2 * f + l], out_ref.at[f, l], in_sem.at[2 * f + l]
                )
            )
    for c in stores:
        c.start()

    @pl.when(jnp.logical_not(at_north))
    def _():
        to_north.wait_send()

    @pl.when(jnp.logical_not(at_south))
    def _():
        to_south.wait_send()

    for c in range(NCH):
        for k in range(G):
            each_x(k, c, lambda d: d.wait_send())

            @pl.when(m != k)
            def _():
                t_copy(k, c).wait_send()

    for c in stores:
        c.wait()


def on_device(fields, w_first, w_second, w_third, w_last):
    vmem = pl.BlockSpec(memory_space=pltpu.VMEM)
    return pl.pallas_call(
        kernel,
        out_shape=jax.ShapeDtypeStruct(fields.shape, F32),
        in_specs=[pl.BlockSpec(memory_space=pl.ANY), vmem, vmem, vmem, vmem],
        out_specs=pl.BlockSpec(memory_space=pl.ANY),
        scratch_shapes=[
            pltpu.VMEM((36, 8, 256), F32),
            pltpu.VMEM((34, 8, 256), F32),
            pltpu.VMEM((34, 8, 256), BF16),
            pltpu.VMEM((SLABS, R, 8, 256), BF16),
            pltpu.VMEM((G, R, 8, 256), BF16),
            pltpu.VMEM((G, R, 8, 256), BF16),
            pltpu.VMEM((32, 8, 256), F32),
            pltpu.VMEM((14 * 64, 64), BF16),
            pltpu.VMEM((6 * 64, 256), BF16),
            pltpu.VMEM((6 * 64, 256), BF16),
            pltpu.VMEM((3, 32, 256), BF16),
            pltpu.VMEM((24, 64), F32),
            pltpu.VMEM((14 * 64, 256), BF16),
            pltpu.VMEM((12 * 64, 256), BF16),
            pltpu.VMEM((10 * 64, 256), BF16),
            pltpu.SemaphoreType.DMA((8,)),
            pltpu.SemaphoreType.DMA((2,)),
            pltpu.SemaphoreType.DMA((2,)),
            pltpu.SemaphoreType.DMA((2, G, NCH)),
            pltpu.SemaphoreType.DMA((SLABS, NCH)),
            pltpu.SemaphoreType.DMA((G, NCH)),
            pltpu.SemaphoreType.DMA((G, NCH)),
        ],
        compiler_params=pltpu.CompilerParams(collective_id=0, has_side_effects=True),
        name="climate_step",
    )(fields, w_first, w_second, w_third, jnp.transpose(w_last, (0, 2, 1)))


def solution(mesh):
    return jax.shard_map(
        on_device,
        mesh=mesh,
        in_specs=(P(None, "wide", "lat", None), P(), P(), P(), P()),
        out_specs=P(None, "wide", "lat", None),
        check_vma=False,
    )
```

```python
import jax
import jax.numpy as jnp
from jax import lax
from jax.experimental import pallas as pl
from jax.experimental.pallas import tpu as pltpu
from jax.sharding import PartitionSpec as P

MESH = pl.DeviceIdType.MESH
F32 = jnp.float32
BF16 = jnp.bfloat16

G = 4
R = 9
STARTS = (0, 8, 17, 25)
CH = 3
NCH = R // CH
SLABS = G + 4


def face_terms(total):
    face = 0.075 * total
    square = face * face + 0.15 * 0.15 * 0.01
    return face, square * lax.rsqrt(square)


def spread(v, first):
    sub = lax.broadcasted_iota(jnp.int32, v.shape, 0)
    if first == 0:
        pair = jnp.where(sub < 2, v, pltpu.roll(v, 2, 0))
    else:
        pair = jnp.where(sub < 2, pltpu.roll(v, 6, 0), v)
    return jnp.where(sub < 4, pair, pltpu.roll(pair, 4, 0))


def transport(rows, masks):
    n = len(rows) - 2
    winds = [spread(v, 2) for v in rows]
    fluxes = []
    for j in range(n + 1):
        low, high = rows[j], rows[j + 1]
        face, speed = face_terms(winds[j] + winds[j + 1])
        flux = face * (low + high) - speed * (high - low)
        if j in masks:
            flux = flux * masks[j]
        fluxes.append(flux)
    outs = []
    for j in range(n):
        cell = rows[j + 1]
        lanes = cell.shape[1]
        wind = spread(cell, 0)
        face, speed = face_terms(wind + pltpu.roll(wind, lanes - 1, 1))
        after = pltpu.roll(cell, lanes - 1, 1)
        flux = face * (cell + after) - speed * (after - cell)
        div = flux - pltpu.roll(flux, 1, 1)
        outs.append(cell - (div + (fluxes[j + 1] - fluxes[j])))
    return outs


def act(t):
    return t + t * jnp.tanh(t)


def dot(a, b):
    return jnp.dot(a, b, preferred_element_type=F32)


def kernel(
    f_hbm, w1_hbm, w2_hbm, w3_hbm, w4_hbm, upd_ref,
    ext, adv, packed, xbuf, tsend, tin, w1_ref, w2_ref, w3_ref, w4_ref,
    wa, wb, band2, band3, wd, stage, h1, h2, h3,
    in_sem, w_sem, halo_send, halo_recv, x_send, x_recv, t_send, t_recv,
):
    lat = lax.axis_index("lat")
    wide = lax.axis_index("wide")
    n_lat = lax.axis_size("lat")
    n_groups = lax.axis_size("wide") // G
    grp = wide // G
    m = wide % G
    at_south = lat == 0
    at_north = lat == n_lat - 1
    up = m >= 2
    og = jnp.where(up, grp + 1, grp - 1)
    os = jnp.where(up, m - 2, m + G + 2)
    has_other = jnp.logical_and(og >= 0, og < n_groups)

    barrier = pltpu.get_barrier_semaphore()

    def greet(la, wi):
        pl.semaphore_signal(barrier, inc=1, device_id=(la, wi), device_id_type=MESH)

    @pl.when(grp > 0)
    def _():
        for k in (2, 3):
            greet(lat, (grp - 1) * G + k)

    @pl.when(grp < n_groups - 1)
    def _():
        for k in (0, 1):
            greet(lat, (grp + 1) * G + k)

    for k in range(G):
        @pl.when(m != k)
        def _():
            greet(lat, grp * G + k)

    @pl.when(jnp.logical_not(at_south))
    def _():
        greet(lat - 1, wide)

    @pl.when(jnp.logical_not(at_north))
    def _():
        greet(lat + 1, wide)

    loads = []
    for f in range(4):
        for l in range(2):
            loads.append(
                pltpu.make_async_copy(
                    f_hbm.at[f, l], ext.at[pl.ds(2, 32), 2 * f + l], in_sem.at[2 * f + l]
                )
            )
    for c in loads:
        c.start()
    w_loads = [
        pltpu.make_async_copy(src, dst, w_sem.at[k])
        for k, (src, dst) in enumerate(
            ((w1_hbm, w1_ref), (w2_hbm, w2_ref), (w3_hbm, w3_ref), (w4_hbm, w4_ref))
        )
    ]
    for c in w_loads:
        c.start()

    @pl.when(at_south)
    def _():
        ext[0:2] = jnp.zeros((2, 8, 256), F32)

    @pl.when(at_north)
    def _():
        ext[34:36] = jnp.zeros((2, 8, 256), F32)

    @pl.when(grp == 0)
    def _():
        xbuf[0:2] = jnp.zeros((2, R, 8, 256), BF16)

    @pl.when(grp == n_groups - 1)
    def _():
        xbuf[G + 2 : G + 4] = jnp.zeros((2, R, 8, 256), BF16)

    for c in loads:
        c.wait()

    def first_body(c, carry):
        e = 2 + 5 * c
        outs = transport([ext[e + i] for i in range(7)], {})
        for i in range(5):
            adv[e + i] = outs[i]
            packed[e + i] = outs[i].astype(BF16)
        return carry

    lax.fori_loop(0, 6, first_body, 0)

    expected = (
        (G - 1)
        + jnp.where(at_south, 0, 1)
        + jnp.where(at_north, 0, 1)
        + jnp.where(has_other, G, 0)
    )
    pl.semaphore_wait(barrier, expected)

    to_north = pltpu.make_async_remote_copy(
        ext.at[pl.ds(32, 2)], ext.at[pl.ds(0, 2)], halo_send.at[0], halo_recv.at[0],
        device_id=(lat + 1, wide), device_id_type=MESH,
    )
    to_south = pltpu.make_async_remote_copy(
        ext.at[pl.ds(2, 2)], ext.at[pl.ds(34, 2)], halo_send.at[1], halo_recv.at[1],
        device_id=(lat - 1, wide), device_id_type=MESH,
    )

    @pl.when(jnp.logical_not(at_north))
    def _():
        to_north.start()

    @pl.when(jnp.logical_not(at_south))
    def _():
        to_south.start()

    def local_row(k, c):
        return (NCH - 1 - c) * CH if k == 0 else c * CH

    def x_copy(k, c, group, slab, sem):
        row = local_row(k, c)
        return pltpu.make_async_remote_copy(
            packed.at[pl.ds(STARTS[k] + row, CH)],
            xbuf.at[slab, pl.ds(row, CH)],
            x_send.at[sem, k, c],
            x_recv.at[slab, c],
            device_id=(lat, group * G + k),
            device_id_type=MESH,
        )

    def each_x(k, c, act_on):
        @pl.when(has_other)
        def _():
            act_on(x_copy(k, c, og, os, 1))

        @pl.when(m != k)
        def _():
            act_on(x_copy(k, c, grp, m + 2, 0))

    for c in range(NCH):
        for k in range(G):
            if c < NCH - 1 or k in (1, 2):
                each_x(k, c, lambda d: d.start())

    @pl.when(jnp.logical_not(at_south))
    def _():
        to_north.wait_recv()

    @pl.when(jnp.logical_not(at_north))
    def _():
        to_south.wait_recv()

    south_open = jnp.where(at_south, 0.0, 1.0).astype(F32)
    north_open = jnp.where(at_north, 0.0, 1.0).astype(F32)
    for e, mask in ((0, south_open), (32, north_open)):
        outs = transport([ext[e + i] for i in range(4)], {1: mask})
        for i in range(2):
            adv[e + i] = outs[i]
            packed[e + i] = outs[i].astype(BF16)
    for k in (0, 3):
        each_x(k, NCH - 1, lambda d: d.start())

    mine = (25 * m + 1) // 3
    xbuf[pl.ds(m + 2, 1)] = packed[pl.ds(mine, R)][None]

    for c in w_loads:
        c.wait()

    def iota(shape, d):
        return lax.broadcasted_iota(jnp.int32, shape, d)

    def one(cond):
        return jnp.where(cond, 1.0, 0.0)

    eye = one(iota((64, 64), 0) == iota((64, 64), 1)).astype(BF16)

    def transposed(w):
        return lax.dot_general(eye, w, (((1,), (1,)), ((), ())), preferred_element_type=F32)

    stage[...] = jnp.zeros((24, 64), F32)
    for k in range(3):
        stage[8 * k : 8 * k + 4] = w1_ref[k].astype(F32)
    w1t = (0.5 * transposed(stage[...].astype(BF16))).astype(BF16)

    def first_band(j, slab, width):
        row = iota((24, width), 0)
        col = iota((24, width), 1)
        same_field = (row & 7) == ((col & 7) >> 1)
        level_in = 2 * (slab + (col >> 3)) + (col & 1)
        band = one(jnp.logical_and(same_field, level_in == j + (row >> 3))).astype(BF16)
        level = 2 * G * grp + j - 3
        valid = jnp.where(
            jnp.logical_and(level >= 0, level < 2 * G * n_groups), 1.0, 0.0
        ).astype(F32)
        return (dot(w1t, band) * valid).astype(BF16)

    for j in range(4, 14):
        wa[64 * (j - 4) : 64 * (j - 3)] = first_band(j, 2, 48)
    for j in range(4):
        wb[64 * j : 64 * j + 64] = first_band(j, 0, 32)
    zeros = jnp.zeros((64, 64), F32)
    for w_ref, band_ref in ((w2_ref, band2), (w3_ref, band3)):
        taps = [0.5 * transposed(w_ref[k]) for k in range(3)]
        for o in range(6):
            off = o - 2
            parts = [taps[i - off] if 0 <= i - off < 3 else zeros for i in range(4)]
            band_ref[64 * o : 64 * o + 64] = jnp.concatenate(parts, axis=1).astype(BF16)
    rho = iota((16, 64), 0)
    level_out = 2 * (rho >> 3) + (rho & 1)
    stage[0:8] = jnp.zeros((8, 64), F32)
    pick = one(iota((16, 8), 1) == ((iota((16, 8), 0) & 7) >> 1)).astype(BF16)
    last = []
    for k in range(3):
        stage[0:4] = w4_ref[k].astype(F32)
        last.append(dot(pick, stage[0:8].astype(BF16)))
    for t in range(2):
        parts = []
        for i in range(4):
            part = jnp.zeros((16, 64), F32)
            for k in range(3):
                part = part + jnp.where(level_out == 4 * t + i - k, last[k], 0.0)
            parts.append(part)
        wd[t] = jnp.concatenate(parts, axis=1).astype(BF16)

    low_valid = jnp.where(grp == 0, 0.0, 1.0).astype(F32)
    high_valid = jnp.where(grp == n_groups - 1, 0.0, 1.0).astype(F32)

    def base_of(c):
        return jnp.where(m == 0, (NCH - 1 - c) * CH, c * CH)

    def t_copy(k, c):
        return pltpu.make_async_remote_copy(
            tsend.at[k, pl.ds(base_of(c), CH)],
            tin.at[m, pl.ds(base_of(c), CH)],
            t_send.at[k, c],
            t_recv.at[m, c],
            device_id=(lat, grp * G + k),
            device_id_type=MESH,
        )

    def x_arrived(s, c):
        pltpu.make_async_remote_copy(
            packed.at[pl.ds(0, CH)], xbuf.at[s, pl.ds(base_of(c), CH)],
            x_send.at[0, 0, c], x_recv.at[s, c], device_id=(lat, wide), device_id_type=MESH,
        ).wait_recv()

    def columns_of(r, first, last):
        parts = [xbuf[s, r].astype(F32) for s in range(first, last)]
        return jnp.concatenate(parts, axis=0).astype(BF16)

    def store_sum(dst, src, r, at, z):
        held = src[r, at + 64 : at + 64 + z.shape[0]].astype(F32)
        dst[r, at : at + z.shape[0]] = (held + act(z)).astype(BF16)

    def upper(c, carry):
        for s in range(2, SLABS):
            cond = grp < n_groups - 1 if s >= G + 2 else m != s - 2

            @pl.when(cond)
            def _():
                x_arrived(s, c)

        rows = [base_of(c) + i for i in range(CH)]
        for r in rows:
            x = columns_of(r, 2, SLABS)
            for q in range(5):
                h1[r, 256 + 128 * q : 384 + 128 * q] = act(
                    dot(wa[128 * q : 128 * q + 128], x)
                ).astype(BF16)
        for r in rows:
            y1 = dot(band2[128:384], h1[r, 256:512])
            y2 = dot(band2[...], h1[r, 512:768])
            y3 = dot(band2[0:128, 0:128], h1[r, 768:896])
            store_sum(h2, h1, r, 256, y1[0:128])
            store_sum(h2, h1, r, 384, y1[128:256] + y2[0:128])
            store_sum(h2, h1, r, 512, y2[128:256])
            store_sum(h2, h1, r, 640, (y2[256:384] + y3) * high_valid)
        for r in rows:
            y1 = dot(band3[128:384], h2[r, 256:512])
            y2 = dot(band3[0:256], h2[r, 512:768])
            store_sum(h3, h2, r, 256, y1[0:128])
            store_sum(h3, h2, r, 384, y1[128:256] + y2[0:128])
            store_sum(h3, h2, r, 512, y2[128:192])
            store_sum(h3, h2, r, 576, y2[192:256] * high_valid)
        for r in rows:
            out = dot(wd[0], h3[r, 256:512]) + dot(wd[1][:, 0:128], h3[r, 512:640])
            for k in (2, 3):
                tsend[k, r] = out[8 * (k - 2) : 8 * (k - 1)].astype(BF16)
        for k in (2, 3):
            @pl.when(m != k)
            def _():
                t_copy(k, c).start()

        return carry

    lax.fori_loop(0, NCH, upper, 0)

    def lower(c, carry):
        for s in (0, 1):
            @pl.when(grp > 0)
            def _():
                x_arrived(s, c)

        rows = [base_of(c) + i for i in range(CH)]
        for r in rows:
            x = columns_of(r, 0, 4)
            for q in range(2):
                h1[r, 128 * q : 128 * q + 128] = act(
                    dot(wb[128 * q : 128 * q + 128], x)
                ).astype(BF16)
        for r in rows:
            y0 = dot(band2[128:384], h1[r, 0:256])
            y1 = dot(band2[0:128, 0:128], h1[r, 256:384])
            store_sum(h2, h1, r, 0, y0[0:128] * low_valid)
            store_sum(h2, h1, r, 128, y0[128:256] + y1)
        for r in rows:
            y0 = dot(band3[128:384], h2[r, 0:256])
            y1 = dot(band3[0:128, 0:128], h2[r, 256:384])
            store_sum(h3, h2, r, 0, y0[0:64] * low_valid)
            store_sum(h3, h2, r, 64, y0[64:128])
            store_sum(h3, h2, r, 128, y0[128:256] + y1)
        for r in rows:
            out = dot(wd[0], h3[r, 0:256]) + dot(wd[1][:, 0:128], h3[r, 256:384])
            for k in (0, 1):
                tsend[k, r] = out[8 * k : 8 * k + 8].astype(BF16)
        for k in (0, 1):
            @pl.when(m != k)
            def _():
                t_copy(k, c).start()

        return carry

    lax.fori_loop(0, NCH, lower, 0)
    tin[pl.ds(m, 1)] = tsend[pl.ds(m, 1)]

    for k in range(G):
        @pl.when(m != k)
        def _():
            for c in range(NCH):
                pltpu.make_async_remote_copy(
                    tsend.at[k, pl.ds(local_row(k, c), CH)],
                    tin.at[k, pl.ds(local_row(k, c), CH)],
                    t_send.at[k, c], t_recv.at[k, c],
                    device_id=(lat, wide), device_id_type=MESH,
                ).wait_recv()

        first = STARTS[k] if k == 0 else STARTS[k - 1] + R
        for e in range(first, STARTS[k] + R):
            upd_ref[e] = adv[e] + tin[k, e - STARTS[k]].astype(F32)

    @pl.when(jnp.logical_not(at_north))
    def _():
        to_north.wait_send()

    @pl.when(jnp.logical_not(at_south))
    def _():
        to_south.wait_send()

    for c in range(NCH):
        for k in range(G):
            each_x(k, c, lambda d: d.wait_send())

            @pl.when(m != k)
            def _():
                t_copy(k, c).wait_send()


def second_kernel(upd_ref, out_ref, outv, sem):
    lat = lax.axis_index("lat")
    at_south = lat == 0
    at_north = lat == lax.axis_size("lat") - 1
    stores = []
    for c in range(4):
        masks = {}
        if c == 0:
            masks = {0: jnp.where(at_south, 0.0, 1.0).astype(F32)}
        if c == 3:
            masks = {8: jnp.where(at_north, 0.0, 1.0).astype(F32)}
        e = 8 * c
        outs = transport([upd_ref[e + i] for i in range(10)], masks)
        for i in range(8):
            outv[e + i] = outs[i]
        for f in range(4):
            for l in range(2):
                d = pltpu.make_async_copy(
                    outv.at[pl.ds(e, 8), 2 * f + l],
                    out_ref.at[f, l, pl.ds(e, 8)],
                    sem.at[c, 2 * f + l],
                )
                d.start()
                stores.append(d)
    for d in stores:
        d.wait()


def on_device(fields, w_first, w_second, w_third, w_last):
    anywhere = pl.BlockSpec(memory_space=pltpu.HBM)
    vmem = pl.BlockSpec(memory_space=pltpu.VMEM)
    dma = pltpu.SemaphoreType.DMA
    updated = pl.pallas_call(
        kernel,
        out_shape=jax.ShapeDtypeStruct((34, 8, 256), F32),
        in_specs=[anywhere] * 5,
        out_specs=vmem,
        scratch_shapes=[
            pltpu.VMEM((36, 8, 256), F32),
            pltpu.VMEM((34, 8, 256), F32),
            pltpu.VMEM((34, 8, 256), BF16),
            pltpu.VMEM((SLABS, R, 8, 256), BF16),
            pltpu.VMEM((G, R, 8, 256), BF16),
            pltpu.VMEM((G, R, 8, 256), BF16),
            pltpu.VMEM((3, 4, 64), BF16),
            pltpu.VMEM((3, 64, 64), BF16),
            pltpu.VMEM((3, 64, 64), BF16),
            pltpu.VMEM((3, 4, 64), BF16),
            pltpu.VMEM((10 * 64, 48), BF16),
            pltpu.VMEM((4 * 64, 32), BF16),
            pltpu.VMEM((6 * 64, 256), BF16),
            pltpu.VMEM((6 * 64, 256), BF16),
            pltpu.VMEM((2, 16, 256), BF16),
            pltpu.VMEM((24, 64), F32),
            pltpu.VMEM((R, 14 * 64, 256), BF16),
            pltpu.VMEM((R, 12 * 64, 256), BF16),
            pltpu.VMEM((R, 10 * 64, 256), BF16),
            dma((8,)),
            dma((4,)),
            dma((2,)),
            dma((2,)),
            dma((2, G, NCH)),
            dma((SLABS, NCH)),
            dma((G, NCH)),
            dma((G, NCH)),
        ],
        compiler_params=pltpu.CompilerParams(
            collective_id=0, has_side_effects=True, vmem_limit_bytes=32 * 1024 * 1024
        ),
        name="climate_step",
        )(*[pltpu.with_memory_space_constraint(v, pltpu.HBM) for v in (fields, w_first, w_second, w_third, jnp.transpose(w_last, (0, 2, 1)))])
    return pl.pallas_call(
        second_kernel,
        out_shape=jax.ShapeDtypeStruct(fields.shape, F32),
        in_specs=[vmem],
        out_specs=anywhere,
        scratch_shapes=[pltpu.VMEM((32, 8, 256), F32), dma((4, 8))],
        compiler_params=pltpu.CompilerParams(vmem_limit_bytes=8 * 1024 * 1024),
        name="climate_end",
    )(updated)


def solution(mesh):
    return jax.shard_map(
        on_device,
        mesh=mesh,
        in_specs=(P(None, "wide", "lat", None), P(), P(), P(), P()),
        out_specs=P(None, "wide", "lat", None),
        check_vma=False,
    )
```

```python
import jax
import jax.numpy as jnp
from jax import lax
from jax.experimental import pallas as pl
from jax.experimental.pallas import tpu as pltpu
from jax.sharding import PartitionSpec as P

MESH = pl.DeviceIdType.MESH
F32 = jnp.float32
BF16 = jnp.bfloat16

G = 4
R = 9
STARTS = (0, 8, 17, 25)
CH = 3
NCH = R // CH
SLABS = G + 4
UPPER = ((0,), (1,), (2,))
LOWER = ((0,), (1,), (2,))


def face_terms(total):
    face = 0.075 * total
    square = face * face + 0.15 * 0.15 * 0.01
    return face, square * lax.rsqrt(square)


def spread(v, first):
    sub = lax.broadcasted_iota(jnp.int32, v.shape, 0)
    if first == 0:
        pair = jnp.where(sub < 2, v, pltpu.roll(v, 2, 0))
    else:
        pair = jnp.where(sub < 2, pltpu.roll(v, 6, 0), v)
    return jnp.where(sub < 4, pair, pltpu.roll(pair, 4, 0))


def transport(rows, masks):
    n = len(rows) - 2
    winds = [spread(v, 2) for v in rows]
    fluxes = []
    for j in range(n + 1):
        low, high = rows[j], rows[j + 1]
        face, speed = face_terms(winds[j] + winds[j + 1])
        flux = face * (low + high) - speed * (high - low)
        if j in masks:
            flux = flux * masks[j]
        fluxes.append(flux)
    outs = []
    for j in range(n):
        cell = rows[j + 1]
        lanes = cell.shape[1]
        wind = spread(cell, 0)
        face, speed = face_terms(wind + pltpu.roll(wind, lanes - 1, 1))
        after = pltpu.roll(cell, lanes - 1, 1)
        flux = face * (cell + after) - speed * (after - cell)
        div = flux - pltpu.roll(flux, 1, 1)
        outs.append(cell - (div + (fluxes[j + 1] - fluxes[j])))
    return outs


def act(t):
    return t + t * jnp.tanh(t)


def dot(a, b):
    return jnp.dot(a, b, preferred_element_type=F32)


def kernel(
    f_hbm, w1_hbm, w2_hbm, w3_hbm, w4_hbm, upd_ref,
    ext, adv, packed, xbuf, tsend, tin, w1_ref, w2_ref, w3_ref, w4_ref,
    band1, band2, band3, wd, stage, h1, h2, h3,
    in_sem, w_sem, halo_send, halo_recv, x_send, x_recv, f_send, f_recv, t_send, t_recv, ready,
):
    lat = lax.axis_index("lat")
    wide = lax.axis_index("wide")
    n_lat = lax.axis_size("lat")
    n_groups = lax.axis_size("wide") // G
    grp = wide // G
    m = wide % G
    at_south = lat == 0
    at_north = lat == n_lat - 1
    has_low = grp > 0
    has_high = grp < n_groups - 1

    barrier = pltpu.get_barrier_semaphore()

    def greet(la, wi):
        pl.semaphore_signal(barrier, inc=1, device_id=(la, wi), device_id_type=MESH)

    @pl.when(has_low)
    def _():
        greet(lat, wide - G)

    for k in range(G):
        @pl.when(m != k)
        def _():
            greet(lat, grp * G + k)

    @pl.when(jnp.logical_not(at_south))
    def _():
        greet(lat - 1, wide)

    @pl.when(jnp.logical_not(at_north))
    def _():
        greet(lat + 1, wide)

    loads = []
    for f in range(4):
        for l in range(2):
            loads.append(
                pltpu.make_async_copy(
                    f_hbm.at[f, l], ext.at[pl.ds(2, 32), 2 * f + l], in_sem.at[2 * f + l]
                )
            )
    for c in loads:
        c.start()
    w_loads = [
        pltpu.make_async_copy(src, dst, w_sem.at[k])
        for k, (src, dst) in enumerate(
            ((w1_hbm, w1_ref), (w2_hbm, w2_ref), (w3_hbm, w3_ref), (w4_hbm, w4_ref))
        )
    ]
    for c in w_loads:
        c.start()

    @pl.when(at_south)
    def _():
        ext[0:2] = jnp.zeros((2, 8, 256), F32)

    @pl.when(at_north)
    def _():
        ext[34:36] = jnp.zeros((2, 8, 256), F32)

    @pl.when(grp == 0)
    def _():
        xbuf[0:2] = jnp.zeros((2, R, 8, 256), BF16)

    @pl.when(grp == n_groups - 1)
    def _():
        xbuf[G + 2 : G + 4] = jnp.zeros((2, R, 8, 256), BF16)

    for c in loads:
        c.wait()

    def local_row(k, c):
        return (NCH - 1 - c) * CH if k == 0 else c * CH

    def base_of(c):
        return jnp.where(m == 0, (NCH - 1 - c) * CH, c * CH)

    def first_transport(k, c, masks):
        e = STARTS[k] + local_row(k, c)
        n = CH - 1 if (k, c) == (2, NCH - 1) else CH
        outs = transport([ext[e + i] for i in range(n + 2)], masks)
        for i in range(n):
            adv[e + i] = outs[i]
            packed[e + i] = outs[i].astype(BF16)

    def x_copy(k, c):
        row = local_row(k, c)
        return pltpu.make_async_remote_copy(
            packed.at[pl.ds(STARTS[k] + row, CH)],
            xbuf.at[m + 2, pl.ds(row, CH)],
            x_send.at[k, c],
            x_recv.at[m, c],
            device_id=(lat, grp * G + k),
            device_id_type=MESH,
        )

    def send_x(k, c):
        @pl.when(m != k)
        def _():
            x_copy(k, c).start()

    for k in range(G):
        first_transport(k, 0, {})

    expected = (
        (G - 1)
        + jnp.where(at_south, 0, 1)
        + jnp.where(at_north, 0, 1)
        + jnp.where(has_high, 1, 0)
    )
    pl.semaphore_wait(barrier, expected)

    @pl.when(has_high)
    def _():
        pl.semaphore_signal(ready, inc=1, device_id=(lat, wide + G), device_id_type=MESH)

    to_north = pltpu.make_async_remote_copy(
        ext.at[pl.ds(32, 2)], ext.at[pl.ds(0, 2)], halo_send.at[0], halo_recv.at[0],
        device_id=(lat + 1, wide), device_id_type=MESH,
    )
    to_south = pltpu.make_async_remote_copy(
        ext.at[pl.ds(2, 2)], ext.at[pl.ds(34, 2)], halo_send.at[1], halo_recv.at[1],
        device_id=(lat - 1, wide), device_id_type=MESH,
    )

    @pl.when(jnp.logical_not(at_north))
    def _():
        to_north.start()

    @pl.when(jnp.logical_not(at_south))
    def _():
        to_south.start()

    for k in range(G):
        send_x(k, 0)
    for k in range(G):
        first_transport(k, 1, {})
    for k in range(G):
        send_x(k, 1)
    for k in (1, 2):
        first_transport(k, NCH - 1, {})
    for k in (1, 2):
        send_x(k, NCH - 1)

    for c in w_loads:
        c.wait()

    def iota(shape, d):
        return lax.broadcasted_iota(jnp.int32, shape, d)

    def one(cond):
        return jnp.where(cond, 1.0, 0.0)

    eye = one(iota((64, 64), 0) == iota((64, 64), 1)).astype(BF16)

    def transposed(w):
        return lax.dot_general(eye, w, (((1,), (1,)), ((), ())), preferred_element_type=F32)

    stage[...] = jnp.zeros((24, 64), F32)
    for k in range(3):
        stage[8 * k : 8 * k + 4] = w1_ref[k].astype(F32)
    w1t = (0.5 * transposed(stage[...].astype(BF16))).astype(BF16)

    row = iota((24, 32), 0)
    col = iota((24, 32), 1)
    same_field = (row & 7) == ((col & 7) >> 1)
    level_in = 2 * (col >> 3) + (col & 1)
    for j in range(6):
        tap = one(jnp.logical_and(same_field, level_in == j + (row >> 3))).astype(BF16)
        band1[64 * j : 64 * j + 64] = dot(w1t, tap).astype(BF16)
    zeros = jnp.zeros((64, 64), F32)
    for w_ref, band_ref in ((w2_ref, band2), (w3_ref, band3)):
        taps = [0.5 * transposed(w_ref[k]) for k in range(3)]
        for o in range(2):
            parts = [taps[i - o] if 0 <= i - o < 3 else zeros for i in range(4)]
            band_ref[64 * o : 64 * o + 64] = jnp.concatenate(parts, axis=1).astype(BF16)
    rho = iota((16, 64), 0)
    level_out = 2 * (rho >> 3) + (rho & 1)
    stage[0:8] = jnp.zeros((8, 64), F32)
    pick = one(iota((16, 8), 1) == ((iota((16, 8), 0) & 7) >> 1)).astype(BF16)
    last = []
    for k in range(3):
        stage[0:4] = w4_ref[k].astype(F32)
        last.append(dot(pick, stage[0:8].astype(BF16)))
    for t in range(2):
        parts = []
        for i in range(4):
            part = jnp.zeros((16, 64), F32)
            for k in range(3):
                part = part + jnp.where(level_out == 4 * t + i - k, last[k], 0.0)
            parts.append(part)
        wd[t] = jnp.concatenate(parts, axis=1).astype(BF16)

    @pl.when(jnp.logical_not(at_south))
    def _():
        to_north.wait_recv()

    @pl.when(jnp.logical_not(at_north))
    def _():
        to_south.wait_recv()

    first_transport(0, NCH - 1, {1: jnp.where(at_south, 0.0, 1.0).astype(F32)})
    first_transport(3, NCH - 1, {2: jnp.where(at_north, 0.0, 1.0).astype(F32)})
    for k in (0, 3):
        send_x(k, NCH - 1)

    def forward(up, c):
        src, dst = (G, 0) if up else (2, G + 2)
        return pltpu.make_async_remote_copy(
            xbuf.at[pl.ds(src, 2), pl.ds(base_of(c), CH)],
            xbuf.at[pl.ds(dst, 2), pl.ds(base_of(c), CH)],
            f_send.at[int(up), c],
            f_recv.at[int(up), c],
            device_id=(lat, wide + G if up else wide - G),
            device_id_type=MESH,
        )

    low_valid = jnp.where(grp == 0, 0.0, 1.0).astype(F32)
    high_valid = jnp.where(grp == n_groups - 1, 0.0, 1.0).astype(F32)

    def t_copy(k, c):
        return pltpu.make_async_remote_copy(
            tsend.at[k, pl.ds(base_of(c), CH)],
            tin.at[m, pl.ds(base_of(c), CH)],
            t_send.at[k, c],
            t_recv.at[m, c],
            device_id=(lat, grp * G + k),
            device_id_type=MESH,
        )

    def store_act(dst, src, at, z, low, high):
        halves = ((0, 128, None),)
        if low is not None or high is not None:
            halves = ((0, 64, low), (64, 64, high))
        for o, size, valid in halves:
            part = z[o : o + size]
            if valid is not None:
                part = part * valid
            out = act(part)
            if src is not None:
                out = src[at + o + 64 : at + o + 64 + size].astype(F32) + out
            dst[at + o : at + o + size] = out.astype(BF16)

    def first_stage(r, slab, pairs, masks):
        parts = [xbuf[s, r].astype(F32) for s in range(slab, slab + 4)]
        x = jnp.concatenate(parts, axis=0).astype(BF16)
        for p in pairs:
            at = 128 * (p - slab)
            z = dot(band1[at : at + 128], x)
            store_act(h1.at[r], None, 128 * p, z, *masks.get(p, (None, None)))

    def later_stage(dst, src, band, r, pairs, masks):
        for p in pairs:
            at = 128 * p
            z = dot(band[...], src[r, at : at + 256])
            store_act(dst.at[r], src.at[r], at, z, *masks.get(p, (None, None)))

    def finish(r, p, members):
        at = 64 * p
        out = dot(wd[0], h3[r, at : at + 256]) + dot(wd[1][:, 0:128], h3[r, at + 256 : at + 384])
        for n, k in enumerate(members):
            tsend[k, r] = out[8 * n : 8 * n + 8].astype(BF16)

    def send_t(members, c):
        for k in members:
            @pl.when(m != k)
            def _():
                t_copy(k, c).start()

    def rows_of(chunks):
        return [base_of(c) + i for c in chunks for i in range(CH)]

    mine = (25 * m + 1) // 3

    def relay(c):
        xbuf[pl.ds(m + 2, 1), pl.ds(base_of(c), CH)] = packed[pl.ds(mine + base_of(c), CH)][None]
        for k in range(G):
            @pl.when(m != k)
            def _():
                pltpu.make_async_remote_copy(
                    packed.at[pl.ds(0, CH)], xbuf.at[k + 2, pl.ds(base_of(c), CH)],
                    x_send.at[k, c], x_recv.at[k, c],
                    device_id=(lat, wide), device_id_type=MESH,
                ).wait_recv()

        @pl.when(has_high)
        def _():
            forward(True, c).start()

        @pl.when(has_low)
        def _():
            if c == 0:
                pl.semaphore_wait(ready, 1)
            forward(False, c).start()

    def middle(c):
        rows = rows_of((c,))
        for r in rows:
            first_stage(r, 2, (2, 3, 4), {})
        for r in rows:
            later_stage(h2, h1, band2, r, (2, 3), {})
        for r in rows:
            later_stage(h3, h2, band3, r, (2,), {})

    relay(0)
    relay(1)
    middle(0)
    relay(2)
    middle(1)
    middle(2)

    def upper(chunks):
        for c in chunks:
            @pl.when(has_high)
            def _():
                forward(False, c).wait_recv()

        rows = rows_of(chunks)
        for r in rows:
            first_stage(r, 4, (5, 6), {5: (None, high_valid), 6: (high_valid, high_valid)})
        for r in rows:
            later_stage(h2, h1, band2, r, (4, 5), {5: (high_valid, high_valid)})
        for r in rows:
            later_stage(h3, h2, band3, r, (3, 4), {4: (None, high_valid)})
        for r in rows:
            finish(r, 4, (2, 3))
        for c in chunks:
            send_t((2, 3), c)

    def lower(chunks):
        for c in chunks:
            @pl.when(has_low)
            def _():
                forward(True, c).wait_recv()

        rows = rows_of(chunks)
        for r in rows:
            first_stage(r, 0, (0, 1), {0: (low_valid, low_valid), 1: (low_valid, None)})
        for r in rows:
            later_stage(h2, h1, band2, r, (0, 1), {0: (low_valid, low_valid)})
        for r in rows:
            later_stage(h3, h2, band3, r, (0, 1), {0: (low_valid, None)})
        for r in rows:
            finish(r, 0, (0, 1))
        for c in chunks:
            send_t((0, 1), c)

    for chunks in UPPER:
        upper(chunks)
    for chunks in LOWER:
        lower(chunks)
    tin[pl.ds(m, 1)] = tsend[pl.ds(m, 1)]

    for k in range(G):
        @pl.when(m != k)
        def _():
            for c in range(NCH):
                pltpu.make_async_remote_copy(
                    tsend.at[k, pl.ds(local_row(k, c), CH)],
                    tin.at[k, pl.ds(local_row(k, c), CH)],
                    t_send.at[k, c], t_recv.at[k, c],
                    device_id=(lat, wide), device_id_type=MESH,
                ).wait_recv()

        first = STARTS[k] if k == 0 else STARTS[k - 1] + R
        for e in range(first, STARTS[k] + R):
            upd_ref[e] = adv[e] + tin[k, e - STARTS[k]].astype(F32)

    @pl.when(jnp.logical_not(at_north))
    def _():
        to_north.wait_send()

    @pl.when(jnp.logical_not(at_south))
    def _():
        to_south.wait_send()

    for c in range(NCH):
        @pl.when(has_high)
        def _():
            forward(True, c).wait_send()

        @pl.when(has_low)
        def _():
            forward(False, c).wait_send()

        for k in range(G):
            @pl.when(m != k)
            def _():
                x_copy(k, c).wait_send()
                t_copy(k, c).wait_send()


def second_kernel(upd_ref, out_ref, outv, sem):
    lat = lax.axis_index("lat")
    at_south = lat == 0
    at_north = lat == lax.axis_size("lat") - 1
    stores = []
    for c in range(4):
        masks = {}
        if c == 0:
            masks = {0: jnp.where(at_south, 0.0, 1.0).astype(F32)}
        if c == 3:
            masks = {8: jnp.where(at_north, 0.0, 1.0).astype(F32)}
        e = 8 * c
        outs = transport([upd_ref[e + i] for i in range(10)], masks)
        for i in range(8):
            outv[e + i] = outs[i]
        for f in range(4):
            for l in range(2):
                d = pltpu.make_async_copy(
                    outv.at[pl.ds(e, 8), 2 * f + l],
                    out_ref.at[f, l, pl.ds(e, 8)],
                    sem.at[c, 2 * f + l],
                )
                d.start()
                stores.append(d)
    for d in stores:
        d.wait()


def on_device(fields, w_first, w_second, w_third, w_last):
    anywhere = pl.BlockSpec(memory_space=pltpu.HBM)
    vmem = pl.BlockSpec(memory_space=pltpu.VMEM)
    dma = pltpu.SemaphoreType.DMA
    arguments = (fields, w_first, w_second, w_third, jnp.transpose(w_last, (0, 2, 1)))
    updated = pl.pallas_call(
        kernel,
        out_shape=jax.ShapeDtypeStruct((34, 8, 256), F32),
        in_specs=[anywhere] * 5,
        out_specs=vmem,
        scratch_shapes=[
            pltpu.VMEM((36, 8, 256), F32),
            pltpu.VMEM((34, 8, 256), F32),
            pltpu.VMEM((34, 8, 256), BF16),
            pltpu.VMEM((SLABS, R, 8, 256), BF16),
            pltpu.VMEM((G, R, 8, 256), BF16),
            pltpu.VMEM((G, R, 8, 256), BF16),
            pltpu.VMEM((3, 4, 64), BF16),
            pltpu.VMEM((3, 64, 64), BF16),
            pltpu.VMEM((3, 64, 64), BF16),
            pltpu.VMEM((3, 4, 64), BF16),
            pltpu.VMEM((6 * 64, 32), BF16),
            pltpu.VMEM((2 * 64, 256), BF16),
            pltpu.VMEM((2 * 64, 256), BF16),
            pltpu.VMEM((2, 16, 256), BF16),
            pltpu.VMEM((24, 64), F32),
            pltpu.VMEM((R, 14 * 64, 256), BF16),
            pltpu.VMEM((R, 12 * 64, 256), BF16),
            pltpu.VMEM((R, 10 * 64, 256), BF16),
            dma((8,)),
            dma((4,)),
            dma((2,)),
            dma((2,)),
            dma((G, NCH)),
            dma((G, NCH)),
            dma((2, NCH)),
            dma((2, NCH)),
            dma((G, NCH)),
            dma((G, NCH)),
            pltpu.SemaphoreType.REGULAR,
        ],
        compiler_params=pltpu.CompilerParams(
            collective_id=0, has_side_effects=True, vmem_limit_bytes=32 * 1024 * 1024
        ),
        name="climate_step",
    )(*[pltpu.with_memory_space_constraint(v, pltpu.HBM) for v in arguments])
    return pl.pallas_call(
        second_kernel,
        out_shape=jax.ShapeDtypeStruct(fields.shape, F32),
        in_specs=[vmem],
        out_specs=anywhere,
        scratch_shapes=[pltpu.VMEM((32, 8, 256), F32), dma((4, 8))],
        compiler_params=pltpu.CompilerParams(vmem_limit_bytes=8 * 1024 * 1024),
        name="climate_end",
    )(updated)


def solution(mesh):
    return jax.shard_map(
        on_device,
        mesh=mesh,
        in_specs=(P(None, "wide", "lat", None), P(), P(), P(), P()),
        out_specs=P(None, "wide", "lat", None),
        check_vma=False,
    )
```

```python
import jax
import jax.numpy as jnp
from jax import lax
from jax.experimental import pallas as pl
from jax.experimental.pallas import tpu as pltpu
from jax.sharding import PartitionSpec as P

MESH = pl.DeviceIdType.MESH
F32 = jnp.float32
BF16 = jnp.bfloat16

G = 4
R = 9
STARTS = (0, 8, 17, 25)
CH = 3
NCH = R // CH
SLABS = G + 4
UPPER = ((0,), (1,), (2,))
LOWER = ((0,), (1,), (2,))


def face_terms(total):
    face = 0.075 * total
    square = face * face + 0.15 * 0.15 * 0.01
    return face, square * lax.rsqrt(square)


def spread(v, first):
    sub = lax.broadcasted_iota(jnp.int32, v.shape, 0)
    if first == 0:
        pair = jnp.where(sub < 2, v, pltpu.roll(v, 2, 0))
    else:
        pair = jnp.where(sub < 2, pltpu.roll(v, 6, 0), v)
    return jnp.where(sub < 4, pair, pltpu.roll(pair, 4, 0))


def transport(rows, masks):
    n = len(rows) - 2
    winds = [spread(v, 2) for v in rows]
    fluxes = []
    for j in range(n + 1):
        low, high = rows[j], rows[j + 1]
        face, speed = face_terms(winds[j] + winds[j + 1])
        flux = face * (low + high) - speed * (high - low)
        if j in masks:
            flux = flux * masks[j]
        fluxes.append(flux)
    outs = []
    for j in range(n):
        cell = rows[j + 1]
        lanes = cell.shape[1]
        wind = spread(cell, 0)
        face, speed = face_terms(wind + pltpu.roll(wind, lanes - 1, 1))
        after = pltpu.roll(cell, lanes - 1, 1)
        flux = face * (cell + after) - speed * (after - cell)
        div = flux - pltpu.roll(flux, 1, 1)
        outs.append(cell - (div + (fluxes[j + 1] - fluxes[j])))
    return outs


def act(t):
    return t + t * jnp.tanh(t)


def dot(a, b):
    return jnp.dot(a, b, preferred_element_type=F32)


def kernel(
    f_hbm, w1_hbm, w2_hbm, w3_hbm, w4_hbm, upd_ref,
    ext, adv, packed, xbuf, tsend, tin, w1_ref, w2_ref, w3_ref, w4_ref,
    band1, band2, band3, wd, stage, h1, h2, h3,
    in_sem, w_sem, halo_send, halo_recv, x_send, x_recv, f_send, f_recv, t_send, t_recv, ready,
):
    lat = lax.axis_index("lat")
    wide = lax.axis_index("wide")
    n_lat = lax.axis_size("lat")
    n_groups = lax.axis_size("wide") // G
    grp = wide // G
    m = wide % G
    at_south = lat == 0
    at_north = lat == n_lat - 1
    has_low = grp > 0
    has_high = grp < n_groups - 1
    cross_low = grp == n_groups // 2
    cross_high = grp == n_groups // 2 - 1
    up = m >= 2
    down = jnp.logical_and(has_low, jnp.logical_not(cross_low))
    has_other = jnp.logical_or(
        jnp.logical_and(up, has_high), jnp.logical_and(jnp.logical_not(up), down)
    )
    og = jnp.where(up, grp + 1, grp - 1)
    os = jnp.where(up, m - 2, m + G + 2)

    barrier = pltpu.get_barrier_semaphore()

    def greet(la, wi):
        pl.semaphore_signal(barrier, inc=1, device_id=(la, wi), device_id_type=MESH)

    @pl.when(has_low)
    def _():
        for k in (2, 3):
            greet(lat, (grp - 1) * G + k)

    @pl.when(jnp.logical_and(has_high, jnp.logical_not(cross_high)))
    def _():
        for k in (0, 1):
            greet(lat, (grp + 1) * G + k)

    @pl.when(jnp.logical_and(cross_low, jnp.logical_not(up)))
    def _():
        greet(lat, wide - G)

    for k in range(G):
        @pl.when(m != k)
        def _():
            greet(lat, grp * G + k)

    @pl.when(jnp.logical_not(at_south))
    def _():
        greet(lat - 1, wide)

    @pl.when(jnp.logical_not(at_north))
    def _():
        greet(lat + 1, wide)

    loads = []
    for f in range(4):
        for l in range(2):
            loads.append(
                pltpu.make_async_copy(
                    f_hbm.at[f, l], ext.at[pl.ds(2, 32), 2 * f + l], in_sem.at[2 * f + l]
                )
            )
    for c in loads:
        c.start()
    w_loads = [
        pltpu.make_async_copy(src, dst, w_sem.at[k])
        for k, (src, dst) in enumerate(
            ((w1_hbm, w1_ref), (w2_hbm, w2_ref), (w3_hbm, w3_ref), (w4_hbm, w4_ref))
        )
    ]
    for c in w_loads:
        c.start()

    @pl.when(at_south)
    def _():
        ext[0:2] = jnp.zeros((2, 8, 256), F32)

    @pl.when(at_north)
    def _():
        ext[34:36] = jnp.zeros((2, 8, 256), F32)

    @pl.when(grp == 0)
    def _():
        xbuf[0:2] = jnp.zeros((2, R, 8, 256), BF16)

    @pl.when(grp == n_groups - 1)
    def _():
        xbuf[G + 2 : G + 4] = jnp.zeros((2, R, 8, 256), BF16)

    for c in loads:
        c.wait()

    def local_row(k, c):
        return (NCH - 1 - c) * CH if k == 0 else c * CH

    def base_of(c):
        return jnp.where(m == 0, (NCH - 1 - c) * CH, c * CH)

    def first_transport(k, c, masks):
        e = STARTS[k] + local_row(k, c)
        n = CH - 1 if (k, c) == (2, NCH - 1) else CH
        outs = transport([ext[e + i] for i in range(n + 2)], masks)
        for i in range(n):
            adv[e + i] = outs[i]
            packed[e + i] = outs[i].astype(BF16)

    def x_copy(k, c, group, slab, other):
        row = local_row(k, c)
        return pltpu.make_async_remote_copy(
            packed.at[pl.ds(STARTS[k] + row, CH)],
            xbuf.at[slab, pl.ds(row, CH)],
            x_send.at[other, k, c],
            x_recv.at[slab, c],
            device_id=(lat, group * G + k),
            device_id_type=MESH,
        )

    def each_x(k, c, act_on):
        @pl.when(has_other)
        def _():
            act_on(x_copy(k, c, og, os, 1))

        @pl.when(m != k)
        def _():
            act_on(x_copy(k, c, grp, m + 2, 0))

    def send_x(k, c):
        each_x(k, c, lambda d: d.start())

    def x_arrived(slab, c):
        pltpu.make_async_remote_copy(
            packed.at[pl.ds(0, CH)], xbuf.at[slab, pl.ds(base_of(c), CH)],
            x_send.at[0, 0, c], x_recv.at[slab, c],
            device_id=(lat, wide), device_id_type=MESH,
        ).wait_recv()

    for k in range(G):
        first_transport(k, 0, {})

    expected = (
        (G - 1)
        + jnp.where(at_south, 0, 1)
        + jnp.where(at_north, 0, 1)
        + jnp.where(has_other, G, 0)
        + jnp.where(jnp.logical_and(cross_high, jnp.logical_not(up)), 1, 0)
    )
    pl.semaphore_wait(barrier, expected)

    @pl.when(cross_high)
    def _():
        pl.semaphore_signal(ready, inc=1, device_id=(lat, wide + G), device_id_type=MESH)

    to_north = pltpu.make_async_remote_copy(
        ext.at[pl.ds(32, 2)], ext.at[pl.ds(0, 2)], halo_send.at[0], halo_recv.at[0],
        device_id=(lat + 1, wide), device_id_type=MESH,
    )
    to_south = pltpu.make_async_remote_copy(
        ext.at[pl.ds(2, 2)], ext.at[pl.ds(34, 2)], halo_send.at[1], halo_recv.at[1],
        device_id=(lat - 1, wide), device_id_type=MESH,
    )

    @pl.when(jnp.logical_not(at_north))
    def _():
        to_north.start()

    @pl.when(jnp.logical_not(at_south))
    def _():
        to_south.start()

    for k in range(G):
        send_x(k, 0)
    for k in range(G):
        first_transport(k, 1, {})
    for k in range(G):
        send_x(k, 1)
    for k in (1, 2):
        first_transport(k, NCH - 1, {})
    for k in (1, 2):
        send_x(k, NCH - 1)

    for c in w_loads:
        c.wait()

    def iota(shape, d):
        return lax.broadcasted_iota(jnp.int32, shape, d)

    def one(cond):
        return jnp.where(cond, 1.0, 0.0)

    eye = one(iota((64, 64), 0) == iota((64, 64), 1)).astype(BF16)

    def transposed(w):
        return lax.dot_general(eye, w, (((1,), (1,)), ((), ())), preferred_element_type=F32)

    stage[...] = jnp.zeros((24, 64), F32)
    for k in range(3):
        stage[8 * k : 8 * k + 4] = w1_ref[k].astype(F32)
    w1t = (0.5 * transposed(stage[...].astype(BF16))).astype(BF16)

    row = iota((24, 32), 0)
    col = iota((24, 32), 1)
    same_field = (row & 7) == ((col & 7) >> 1)
    level_in = 2 * (col >> 3) + (col & 1)
    for j in range(6):
        tap = one(jnp.logical_and(same_field, level_in == j + (row >> 3))).astype(BF16)
        band1[64 * j : 64 * j + 64] = dot(w1t, tap).astype(BF16)
    zeros = jnp.zeros((64, 64), F32)
    for w_ref, band_ref in ((w2_ref, band2), (w3_ref, band3)):
        taps = [0.5 * transposed(w_ref[k]) for k in range(3)]
        for o in range(2):
            parts = [taps[i - o] if 0 <= i - o < 3 else zeros for i in range(4)]
            band_ref[64 * o : 64 * o + 64] = jnp.concatenate(parts, axis=1).astype(BF16)
    rho = iota((16, 64), 0)
    level_out = 2 * (rho >> 3) + (rho & 1)
    stage[0:8] = jnp.zeros((8, 64), F32)
    pick = one(iota((16, 8), 1) == ((iota((16, 8), 0) & 7) >> 1)).astype(BF16)
    last = []
    for k in range(3):
        stage[0:4] = w4_ref[k].astype(F32)
        last.append(dot(pick, stage[0:8].astype(BF16)))
    for t in range(2):
        parts = []
        for i in range(4):
            part = jnp.zeros((16, 64), F32)
            for k in range(3):
                part = part + jnp.where(level_out == 4 * t + i - k, last[k], 0.0)
            parts.append(part)
        wd[t] = jnp.concatenate(parts, axis=1).astype(BF16)

    @pl.when(jnp.logical_not(at_south))
    def _():
        to_north.wait_recv()

    @pl.when(jnp.logical_not(at_north))
    def _():
        to_south.wait_recv()

    first_transport(0, NCH - 1, {1: jnp.where(at_south, 0.0, 1.0).astype(F32)})
    first_transport(3, NCH - 1, {2: jnp.where(at_north, 0.0, 1.0).astype(F32)})
    for k in (0, 3):
        send_x(k, NCH - 1)

    def forward(c):
        return pltpu.make_async_remote_copy(
            xbuf.at[pl.ds(2, 2), pl.ds(base_of(c), CH)],
            xbuf.at[pl.ds(G + 2, 2), pl.ds(base_of(c), CH)],
            f_send.at[c],
            f_recv.at[c],
            device_id=(lat, wide - G),
            device_id_type=MESH,
        )

    low_valid = jnp.where(grp == 0, 0.0, 1.0).astype(F32)
    high_valid = jnp.where(grp == n_groups - 1, 0.0, 1.0).astype(F32)

    def t_copy(k, c):
        return pltpu.make_async_remote_copy(
            tsend.at[k, pl.ds(base_of(c), CH)],
            tin.at[m, pl.ds(base_of(c), CH)],
            t_send.at[k, c],
            t_recv.at[m, c],
            device_id=(lat, grp * G + k),
            device_id_type=MESH,
        )

    def store_act(dst, src, at, z, low, high):
        halves = ((0, 128, None),)
        if low is not None or high is not None:
            halves = ((0, 64, low), (64, 64, high))
        for o, size, valid in halves:
            part = z[o : o + size]
            if valid is not None:
                part = part * valid
            out = act(part)
            if src is not None:
                out = src[at + o + 64 : at + o + 64 + size].astype(F32) + out
            dst[at + o : at + o + size] = out.astype(BF16)

    def first_stage(r, slab, pairs, masks):
        parts = [xbuf[s, r].astype(F32) for s in range(slab, slab + 4)]
        x = jnp.concatenate(parts, axis=0).astype(BF16)
        for p in pairs:
            at = 128 * (p - slab)
            z = dot(band1[at : at + 128], x)
            store_act(h1.at[r], None, 128 * p, z, *masks.get(p, (None, None)))

    def later_stage(dst, src, band, r, pairs, masks):
        for p in pairs:
            at = 128 * p
            z = dot(band[...], src[r, at : at + 256])
            store_act(dst.at[r], src.at[r], at, z, *masks.get(p, (None, None)))

    def finish(r, p, members):
        at = 64 * p
        out = dot(wd[0], h3[r, at : at + 256]) + dot(wd[1][:, 0:128], h3[r, at + 256 : at + 384])
        for n, k in enumerate(members):
            tsend[k, r] = out[8 * n : 8 * n + 8].astype(BF16)

    def send_t(members, c):
        for k in members:
            @pl.when(m != k)
            def _():
                t_copy(k, c).start()

    def rows_of(chunks):
        return [base_of(c) + i for c in chunks for i in range(CH)]

    mine = (25 * m + 1) // 3

    def relay(c):
        xbuf[pl.ds(m + 2, 1), pl.ds(base_of(c), CH)] = packed[pl.ds(mine + base_of(c), CH)][None]
        for k in range(G):
            @pl.when(m != k)
            def _():
                x_arrived(k + 2, c)

        @pl.when(cross_low)
        def _():
            if c == 0:
                pl.semaphore_wait(ready, 1)
            forward(c).start()

    def middle(c):
        rows = rows_of((c,))
        for r in rows:
            first_stage(r, 2, (2, 3, 4), {})
        for r in rows:
            later_stage(h2, h1, band2, r, (2, 3), {})
        for r in rows:
            later_stage(h3, h2, band3, r, (2,), {})

    relay(0)
    relay(1)
    middle(0)
    relay(2)
    middle(1)
    middle(2)

    def upper(chunks):
        for c in chunks:
            @pl.when(cross_high)
            def _():
                forward(c).wait_recv()

            @pl.when(jnp.logical_and(has_high, jnp.logical_not(cross_high)))
            def _():
                x_arrived(G + 2, c)
                x_arrived(G + 3, c)

        rows = rows_of(chunks)
        for r in rows:
            first_stage(r, 4, (5, 6), {5: (None, high_valid), 6: (high_valid, high_valid)})
        for r in rows:
            later_stage(h2, h1, band2, r, (4, 5), {5: (high_valid, high_valid)})
        for r in rows:
            later_stage(h3, h2, band3, r, (3, 4), {4: (None, high_valid)})
        for r in rows:
            finish(r, 4, (2, 3))
        for c in chunks:
            send_t((2, 3), c)

    def lower(chunks):
        for c in chunks:
            @pl.when(has_low)
            def _():
                x_arrived(0, c)
                x_arrived(1, c)

        rows = rows_of(chunks)
        for r in rows:
            first_stage(r, 0, (0, 1), {0: (low_valid, low_valid), 1: (low_valid, None)})
        for r in rows:
            later_stage(h2, h1, band2, r, (0, 1), {0: (low_valid, low_valid)})
        for r in rows:
            later_stage(h3, h2, band3, r, (0, 1), {0: (low_valid, None)})
        for r in rows:
            finish(r, 0, (0, 1))
        for c in chunks:
            send_t((0, 1), c)

    for chunks in UPPER:
        upper(chunks)
    for chunks in LOWER:
        lower(chunks)
    tin[pl.ds(m, 1)] = tsend[pl.ds(m, 1)]

    for k in range(G):
        @pl.when(m != k)
        def _():
            for c in range(NCH):
                pltpu.make_async_remote_copy(
                    tsend.at[k, pl.ds(local_row(k, c), CH)],
                    tin.at[k, pl.ds(local_row(k, c), CH)],
                    t_send.at[k, c], t_recv.at[k, c],
                    device_id=(lat, wide), device_id_type=MESH,
                ).wait_recv()

        first = STARTS[k] if k == 0 else STARTS[k - 1] + R
        for e in range(first, STARTS[k] + R):
            upd_ref[e] = adv[e] + tin[k, e - STARTS[k]].astype(F32)

    @pl.when(jnp.logical_not(at_north))
    def _():
        to_north.wait_send()

    @pl.when(jnp.logical_not(at_south))
    def _():
        to_south.wait_send()

    for c in range(NCH):
        @pl.when(cross_low)
        def _():
            forward(c).wait_send()

        for k in range(G):
            each_x(k, c, lambda d: d.wait_send())

            @pl.when(m != k)
            def _():
                t_copy(k, c).wait_send()


def second_kernel(upd_ref, out_ref, outv, sem):
    lat = lax.axis_index("lat")
    at_south = lat == 0
    at_north = lat == lax.axis_size("lat") - 1
    stores = []
    for c in range(4):
        masks = {}
        if c == 0:
            masks = {0: jnp.where(at_south, 0.0, 1.0).astype(F32)}
        if c == 3:
            masks = {8: jnp.where(at_north, 0.0, 1.0).astype(F32)}
        e = 8 * c
        outs = transport([upd_ref[e + i] for i in range(10)], masks)
        for i in range(8):
            outv[e + i] = outs[i]
        for f in range(4):
            for l in range(2):
                d = pltpu.make_async_copy(
                    outv.at[pl.ds(e, 8), 2 * f + l],
                    out_ref.at[f, l, pl.ds(e, 8)],
                    sem.at[c, 2 * f + l],
                )
                d.start()
                stores.append(d)
    for d in stores:
        d.wait()


def on_device(fields, w_first, w_second, w_third, w_last):
    anywhere = pl.BlockSpec(memory_space=pltpu.HBM)
    vmem = pl.BlockSpec(memory_space=pltpu.VMEM)
    dma = pltpu.SemaphoreType.DMA
    arguments = (fields, w_first, w_second, w_third, jnp.transpose(w_last, (0, 2, 1)))
    updated = pl.pallas_call(
        kernel,
        out_shape=jax.ShapeDtypeStruct((34, 8, 256), F32),
        in_specs=[anywhere] * 5,
        out_specs=vmem,
        scratch_shapes=[
            pltpu.VMEM((36, 8, 256), F32),
            pltpu.VMEM((34, 8, 256), F32),
            pltpu.VMEM((34, 8, 256), BF16),
            pltpu.VMEM((SLABS, R, 8, 256), BF16),
            pltpu.VMEM((G, R, 8, 256), BF16),
            pltpu.VMEM((G, R, 8, 256), BF16),
            pltpu.VMEM((3, 4, 64), BF16),
            pltpu.VMEM((3, 64, 64), BF16),
            pltpu.VMEM((3, 64, 64), BF16),
            pltpu.VMEM((3, 4, 64), BF16),
            pltpu.VMEM((6 * 64, 32), BF16),
            pltpu.VMEM((2 * 64, 256), BF16),
            pltpu.VMEM((2 * 64, 256), BF16),
            pltpu.VMEM((2, 16, 256), BF16),
            pltpu.VMEM((24, 64), F32),
            pltpu.VMEM((R, 14 * 64, 256), BF16),
            pltpu.VMEM((R, 12 * 64, 256), BF16),
            pltpu.VMEM((R, 10 * 64, 256), BF16),
            dma((8,)),
            dma((4,)),
            dma((2,)),
            dma((2,)),
            dma((2, G, NCH)),
            dma((SLABS, NCH)),
            dma((NCH,)),
            dma((NCH,)),
            dma((G, NCH)),
            dma((G, NCH)),
            pltpu.SemaphoreType.REGULAR,
        ],
        compiler_params=pltpu.CompilerParams(
            collective_id=0, has_side_effects=True, vmem_limit_bytes=32 * 1024 * 1024
        ),
        name="climate_step",
    )(*[pltpu.with_memory_space_constraint(v, pltpu.HBM) for v in arguments])
    return pl.pallas_call(
        second_kernel,
        out_shape=jax.ShapeDtypeStruct(fields.shape, F32),
        in_specs=[vmem],
        out_specs=anywhere,
        scratch_shapes=[pltpu.VMEM((32, 8, 256), F32), dma((4, 8))],
        compiler_params=pltpu.CompilerParams(vmem_limit_bytes=8 * 1024 * 1024),
        name="climate_end",
    )(updated)


def solution(mesh):
    return jax.shard_map(
        on_device,
        mesh=mesh,
        in_specs=(P(None, "wide", "lat", None), P(), P(), P(), P()),
        out_specs=P(None, "wide", "lat", None),
        check_vma=False,
    )
```

```python
import jax
import jax.numpy as jnp
from jax import lax
from jax.experimental import pallas as pl
from jax.experimental.pallas import tpu as pltpu
from jax.sharding import PartitionSpec as P

MESH = pl.DeviceIdType.MESH
F32 = jnp.float32
BF16 = jnp.bfloat16

G = 4
R = 9
STARTS = (0, 8, 17, 25)
CH = 3
NCH = R // CH
SLABS = G + 4
UPPER = ((0, 1, 2),)
LOWER = ((0,), (1,), (2,))


def face_terms(total):
    face = 0.075 * total
    square = face * face + 0.15 * 0.15 * 0.01
    return face, square * lax.rsqrt(square)


def spread(v, first):
    sub = lax.broadcasted_iota(jnp.int32, v.shape, 0)
    if first == 0:
        pair = jnp.where(sub < 2, v, pltpu.roll(v, 2, 0))
    else:
        pair = jnp.where(sub < 2, pltpu.roll(v, 6, 0), v)
    return jnp.where(sub < 4, pair, pltpu.roll(pair, 4, 0))


def transport(rows, masks):
    n = len(rows) - 2
    winds = [spread(v, 2) for v in rows]
    fluxes = []
    for j in range(n + 1):
        low, high = rows[j], rows[j + 1]
        face, speed = face_terms(winds[j] + winds[j + 1])
        flux = face * (low + high) - speed * (high - low)
        if j in masks:
            flux = flux * masks[j]
        fluxes.append(flux)
    outs = []
    for j in range(n):
        cell = rows[j + 1]
        lanes = cell.shape[1]
        wind = spread(cell, 0)
        face, speed = face_terms(wind + pltpu.roll(wind, lanes - 1, 1))
        after = pltpu.roll(cell, lanes - 1, 1)
        flux = face * (cell + after) - speed * (after - cell)
        div = flux - pltpu.roll(flux, 1, 1)
        outs.append(cell - (div + (fluxes[j + 1] - fluxes[j])))
    return outs


def act(t):
    return t + t * jnp.tanh(t)


def dot(a, b):
    return jnp.dot(a, b, preferred_element_type=F32)


def kernel(
    f_hbm, w1_hbm, w2_hbm, w3_hbm, w4_hbm, upd_ref,
    ext, adv, packed, xbuf, tsend, tin, w1_ref, w2_ref, w3_ref, w4_ref,
    band1, band2, band3, wd, stage, h1, h2, h3,
    in_sem, w_sem, halo_send, halo_recv, x_send, x_recv, f_send, f_recv, t_send, t_recv, ready,
):
    lat = lax.axis_index("lat")
    wide = lax.axis_index("wide")
    n_lat = lax.axis_size("lat")
    n_groups = lax.axis_size("wide") // G
    grp = wide // G
    m = wide % G
    at_south = lat == 0
    at_north = lat == n_lat - 1
    has_low = grp > 0
    has_high = grp < n_groups - 1
    cross_low = grp == n_groups // 2
    cross_high = grp == n_groups // 2 - 1
    up = m >= 2
    down = jnp.logical_and(has_low, jnp.logical_not(cross_low))
    has_other = jnp.logical_or(
        jnp.logical_and(up, has_high), jnp.logical_and(jnp.logical_not(up), down)
    )
    og = jnp.where(up, grp + 1, grp - 1)
    os = jnp.where(up, m - 2, m + G + 2)

    barrier = pltpu.get_barrier_semaphore()

    def greet(la, wi):
        pl.semaphore_signal(barrier, inc=1, device_id=(la, wi), device_id_type=MESH)

    @pl.when(has_low)
    def _():
        for k in (2, 3):
            greet(lat, (grp - 1) * G + k)

    @pl.when(jnp.logical_and(has_high, jnp.logical_not(cross_high)))
    def _():
        for k in (0, 1):
            greet(lat, (grp + 1) * G + k)

    @pl.when(jnp.logical_and(cross_low, jnp.logical_not(up)))
    def _():
        greet(lat, wide - G)

    for k in range(G):
        @pl.when(m != k)
        def _():
            greet(lat, grp * G + k)

    @pl.when(jnp.logical_not(at_south))
    def _():
        greet(lat - 1, wide)

    @pl.when(jnp.logical_not(at_north))
    def _():
        greet(lat + 1, wide)

    loads = []
    for f in range(4):
        for l in range(2):
            loads.append(
                pltpu.make_async_copy(
                    f_hbm.at[f, l], ext.at[pl.ds(2, 32), 2 * f + l], in_sem.at[2 * f + l]
                )
            )
    for c in loads:
        c.start()
    w_loads = [
        pltpu.make_async_copy(src, dst, w_sem.at[k])
        for k, (src, dst) in enumerate(
            ((w1_hbm, w1_ref), (w2_hbm, w2_ref), (w3_hbm, w3_ref), (w4_hbm, w4_ref))
        )
    ]
    for c in w_loads:
        c.start()

    @pl.when(at_south)
    def _():
        ext[0:2] = jnp.zeros((2, 8, 256), F32)

    @pl.when(at_north)
    def _():
        ext[34:36] = jnp.zeros((2, 8, 256), F32)

    @pl.when(grp == 0)
    def _():
        xbuf[0:2] = jnp.zeros((2, R, 8, 256), BF16)

    @pl.when(grp == n_groups - 1)
    def _():
        xbuf[G + 2 : G + 4] = jnp.zeros((2, R, 8, 256), BF16)

    for c in loads:
        c.wait()

    def local_row(k, c):
        return (NCH - 1 - c) * CH if k == 0 else c * CH

    def base_of(c):
        return jnp.where(m == 0, (NCH - 1 - c) * CH, c * CH)

    def first_transport(k, c, masks):
        e = STARTS[k] + local_row(k, c)
        n = CH - 1 if (k, c) == (2, NCH - 1) else CH
        outs = transport([ext[e + i] for i in range(n + 2)], masks)
        for i in range(n):
            adv[e + i] = outs[i]
            packed[e + i] = outs[i].astype(BF16)

    def x_copy(k, c, group, slab, other):
        row = local_row(k, c)
        return pltpu.make_async_remote_copy(
            packed.at[pl.ds(STARTS[k] + row, CH)],
            xbuf.at[slab, pl.ds(row, CH)],
            x_send.at[other, k, c],
            x_recv.at[slab, c],
            device_id=(lat, group * G + k),
            device_id_type=MESH,
        )

    def each_x(k, c, act_on):
        @pl.when(has_other)
        def _():
            act_on(x_copy(k, c, og, os, 1))

        @pl.when(m != k)
        def _():
            act_on(x_copy(k, c, grp, m + 2, 0))

    def send_x(k, c):
        each_x(k, c, lambda d: d.start())

    def x_arrived(slab, c):
        pltpu.make_async_remote_copy(
            packed.at[pl.ds(0, CH)], xbuf.at[slab, pl.ds(base_of(c), CH)],
            x_send.at[0, 0, c], x_recv.at[slab, c],
            device_id=(lat, wide), device_id_type=MESH,
        ).wait_recv()

    for k in range(G):
        first_transport(k, 0, {})

    expected = (
        (G - 1)
        + jnp.where(at_south, 0, 1)
        + jnp.where(at_north, 0, 1)
        + jnp.where(has_other, G, 0)
        + jnp.where(jnp.logical_and(cross_high, jnp.logical_not(up)), 1, 0)
    )
    pl.semaphore_wait(barrier, expected)

    @pl.when(cross_high)
    def _():
        pl.semaphore_signal(ready, inc=1, device_id=(lat, wide + G), device_id_type=MESH)

    to_north = pltpu.make_async_remote_copy(
        ext.at[pl.ds(32, 2)], ext.at[pl.ds(0, 2)], halo_send.at[0], halo_recv.at[0],
        device_id=(lat + 1, wide), device_id_type=MESH,
    )
    to_south = pltpu.make_async_remote_copy(
        ext.at[pl.ds(2, 2)], ext.at[pl.ds(34, 2)], halo_send.at[1], halo_recv.at[1],
        device_id=(lat - 1, wide), device_id_type=MESH,
    )

    @pl.when(jnp.logical_not(at_north))
    def _():
        to_north.start()

    @pl.when(jnp.logical_not(at_south))
    def _():
        to_south.start()

    for k in range(G):
        send_x(k, 0)
    for k in range(G):
        first_transport(k, 1, {})
    for k in range(G):
        send_x(k, 1)
    for k in (1, 2):
        first_transport(k, NCH - 1, {})
    for k in (1, 2):
        send_x(k, NCH - 1)

    for c in w_loads:
        c.wait()

    def iota(shape, d):
        return lax.broadcasted_iota(jnp.int32, shape, d)

    def one(cond):
        return jnp.where(cond, 1.0, 0.0)

    eye = one(iota((64, 64), 0) == iota((64, 64), 1)).astype(BF16)

    def transposed(w):
        return lax.dot_general(eye, w, (((1,), (1,)), ((), ())), preferred_element_type=F32)

    stage[...] = jnp.zeros((24, 64), F32)
    for k in range(3):
        stage[8 * k : 8 * k + 4] = w1_ref[k].astype(F32)
    w1t = (0.5 * transposed(stage[...].astype(BF16))).astype(BF16)

    row = iota((24, 32), 0)
    col = iota((24, 32), 1)
    same_field = (row & 7) == ((col & 7) >> 1)
    level_in = 2 * (col >> 3) + (col & 1)
    for j in range(6):
        tap = one(jnp.logical_and(same_field, level_in == j + (row >> 3))).astype(BF16)
        band1[64 * j : 64 * j + 64] = dot(w1t, tap).astype(BF16)
    zeros = jnp.zeros((64, 64), F32)
    for w_ref, band_ref in ((w2_ref, band2), (w3_ref, band3)):
        taps = [0.5 * transposed(w_ref[k]) for k in range(3)]
        for o in range(2):
            parts = [taps[i - o] if 0 <= i - o < 3 else zeros for i in range(4)]
            band_ref[64 * o : 64 * o + 64] = jnp.concatenate(parts, axis=1).astype(BF16)
    rho = iota((16, 64), 0)
    level_out = 2 * (rho >> 3) + (rho & 1)
    stage[0:8] = jnp.zeros((8, 64), F32)
    pick = one(iota((16, 8), 1) == ((iota((16, 8), 0) & 7) >> 1)).astype(BF16)
    last = []
    for k in range(3):
        stage[0:4] = w4_ref[k].astype(F32)
        last.append(dot(pick, stage[0:8].astype(BF16)))
    for t in range(2):
        parts = []
        for i in range(4):
            part = jnp.zeros((16, 64), F32)
            for k in range(3):
                part = part + jnp.where(level_out == 4 * t + i - k, last[k], 0.0)
            parts.append(part)
        wd[t] = jnp.concatenate(parts, axis=1).astype(BF16)

    @pl.when(jnp.logical_not(at_south))
    def _():
        to_north.wait_recv()

    @pl.when(jnp.logical_not(at_north))
    def _():
        to_south.wait_recv()

    first_transport(0, NCH - 1, {1: jnp.where(at_south, 0.0, 1.0).astype(F32)})
    first_transport(3, NCH - 1, {2: jnp.where(at_north, 0.0, 1.0).astype(F32)})
    for k in (0, 3):
        send_x(k, NCH - 1)

    def forward(c):
        return pltpu.make_async_remote_copy(
            xbuf.at[pl.ds(2, 2), pl.ds(base_of(c), CH)],
            xbuf.at[pl.ds(G + 2, 2), pl.ds(base_of(c), CH)],
            f_send.at[c],
            f_recv.at[c],
            device_id=(lat, wide - G),
            device_id_type=MESH,
        )

    low_valid = jnp.where(grp == 0, 0.0, 1.0).astype(F32)
    high_valid = jnp.where(grp == n_groups - 1, 0.0, 1.0).astype(F32)

    def t_copy(k, c):
        return pltpu.make_async_remote_copy(
            tsend.at[k, pl.ds(base_of(c), CH)],
            tin.at[m, pl.ds(base_of(c), CH)],
            t_send.at[k, c],
            t_recv.at[m, c],
            device_id=(lat, grp * G + k),
            device_id_type=MESH,
        )

    def store_act(dst, src, at, z, low, high):
        halves = ((0, 128, None),)
        if low is not None or high is not None:
            halves = ((0, 64, low), (64, 64, high))
        for o, size, valid in halves:
            part = z[o : o + size]
            if valid is not None:
                part = part * valid
            out = act(part)
            if src is not None:
                out = src[at + o + 64 : at + o + 64 + size].astype(F32) + out
            dst[at + o : at + o + size] = out.astype(BF16)

    def first_stage(row, slab, pairs, masks):
        r, at_row = row
        parts = [xbuf[s, r].astype(F32) for s in range(slab, slab + 4)]
        x = jnp.concatenate(parts, axis=0).astype(BF16)
        for p in pairs:
            at = 128 * (p - slab)
            z = dot(band1[at : at + 128], x)
            store_act(h1.at[at_row], None, 128 * p, z, *masks.get(p, (None, None)))

    def later_stage(dst, src, band, row, pairs, masks):
        for p in pairs:
            at = 128 * p
            z = dot(band[...], src[row[1], at : at + 256])
            store_act(dst.at[row[1]], src.at[row[1]], at, z, *masks.get(p, (None, None)))

    def finish(row, p, members):
        r, n_row = row
        at = 64 * p
        out = dot(wd[0], h3[n_row, at : at + 256]) + dot(wd[1][:, 0:128], h3[n_row, at + 256 : at + 384])
        for n, k in enumerate(members):
            tsend[k, r] = out[8 * n : 8 * n + 8].astype(BF16)

    def send_t(members, c):
        for k in members:
            @pl.when(m != k)
            def _():
                t_copy(k, c).start()

    def rows_of(chunks):
        return [(base_of(c) + i, CH * c + i) for c in chunks for i in range(CH)]

    mine = (25 * m + 1) // 3

    def relay(c):
        xbuf[pl.ds(m + 2, 1), pl.ds(base_of(c), CH)] = packed[pl.ds(mine + base_of(c), CH)][None]
        for k in range(G):
            @pl.when(m != k)
            def _():
                x_arrived(k + 2, c)

        @pl.when(cross_low)
        def _():
            if c == 0:
                pl.semaphore_wait(ready, 1)
            forward(c).start()

    def middle(c):
        rows = rows_of((c,))
        for r in rows:
            first_stage(r, 2, (2, 3, 4), {})
        for r in rows:
            later_stage(h2, h1, band2, r, (2, 3), {})
        for r in rows:
            later_stage(h3, h2, band3, r, (2,), {})

    relay(0)
    relay(1)
    middle(0)
    relay(2)
    middle(1)
    middle(2)

    def upper(chunks):
        for c in chunks:
            @pl.when(cross_high)
            def _():
                forward(c).wait_recv()

            @pl.when(jnp.logical_and(has_high, jnp.logical_not(cross_high)))
            def _():
                x_arrived(G + 2, c)
                x_arrived(G + 3, c)

        rows = rows_of(chunks)
        for r in rows:
            first_stage(r, 4, (5, 6), {5: (None, high_valid), 6: (high_valid, high_valid)})
        for r in rows:
            later_stage(h2, h1, band2, r, (4, 5), {5: (high_valid, high_valid)})
        for r in rows:
            later_stage(h3, h2, band3, r, (3, 4), {4: (None, high_valid)})
        for r in rows:
            finish(r, 4, (2, 3))
        for c in chunks:
            send_t((2, 3), c)

    def lower(chunks):
        for c in chunks:
            @pl.when(has_low)
            def _():
                x_arrived(0, c)
                x_arrived(1, c)

        rows = rows_of(chunks)
        for r in rows:
            first_stage(r, 0, (0, 1), {0: (low_valid, low_valid), 1: (low_valid, None)})
        for r in rows:
            later_stage(h2, h1, band2, r, (0, 1), {0: (low_valid, low_valid)})
        for r in rows:
            later_stage(h3, h2, band3, r, (0, 1), {0: (low_valid, None)})
        for r in rows:
            finish(r, 0, (0, 1))
        for c in chunks:
            send_t((0, 1), c)

    for chunks in UPPER:
        upper(chunks)
    for chunks in LOWER:
        lower(chunks)
    tin[pl.ds(m, 1)] = tsend[pl.ds(m, 1)]

    for k in range(G):
        @pl.when(m != k)
        def _():
            for c in range(NCH):
                pltpu.make_async_remote_copy(
                    tsend.at[k, pl.ds(local_row(k, c), CH)],
                    tin.at[k, pl.ds(local_row(k, c), CH)],
                    t_send.at[k, c], t_recv.at[k, c],
                    device_id=(lat, wide), device_id_type=MESH,
                ).wait_recv()

        first = STARTS[k] if k == 0 else STARTS[k - 1] + R
        for e in range(first, STARTS[k] + R):
            upd_ref[e] = adv[e] + tin[k, e - STARTS[k]].astype(F32)

    @pl.when(jnp.logical_not(at_north))
    def _():
        to_north.wait_send()

    @pl.when(jnp.logical_not(at_south))
    def _():
        to_south.wait_send()

    for c in range(NCH):
        @pl.when(cross_low)
        def _():
            forward(c).wait_send()

        for k in range(G):
            each_x(k, c, lambda d: d.wait_send())

            @pl.when(m != k)
            def _():
                t_copy(k, c).wait_send()


def second_kernel(upd_ref, out_ref, outv, sem):
    lat = lax.axis_index("lat")
    at_south = lat == 0
    at_north = lat == lax.axis_size("lat") - 1
    stores = []
    for c in range(4):
        masks = {}
        if c == 0:
            masks = {0: jnp.where(at_south, 0.0, 1.0).astype(F32)}
        if c == 3:
            masks = {8: jnp.where(at_north, 0.0, 1.0).astype(F32)}
        e = 8 * c
        outs = transport([upd_ref[e + i] for i in range(10)], masks)
        for i in range(8):
            outv[e + i] = outs[i]
        for f in range(4):
            for l in range(2):
                d = pltpu.make_async_copy(
                    outv.at[pl.ds(e, 8), 2 * f + l],
                    out_ref.at[f, l, pl.ds(e, 8)],
                    sem.at[c, 2 * f + l],
                )
                d.start()
                stores.append(d)
    for d in stores:
        d.wait()


def on_device(fields, w_first, w_second, w_third, w_last):
    anywhere = pl.BlockSpec(memory_space=pltpu.HBM)
    vmem = pl.BlockSpec(memory_space=pltpu.VMEM)
    dma = pltpu.SemaphoreType.DMA
    arguments = (fields, w_first, w_second, w_third, jnp.transpose(w_last, (0, 2, 1)))
    updated = pl.pallas_call(
        kernel,
        out_shape=jax.ShapeDtypeStruct((34, 8, 256), F32),
        in_specs=[anywhere] * 5,
        out_specs=vmem,
        scratch_shapes=[
            pltpu.VMEM((36, 8, 256), F32),
            pltpu.VMEM((34, 8, 256), F32),
            pltpu.VMEM((34, 8, 256), BF16),
            pltpu.VMEM((SLABS, R, 8, 256), BF16),
            pltpu.VMEM((G, R, 8, 256), BF16),
            pltpu.VMEM((G, R, 8, 256), BF16),
            pltpu.VMEM((3, 4, 64), BF16),
            pltpu.VMEM((3, 64, 64), BF16),
            pltpu.VMEM((3, 64, 64), BF16),
            pltpu.VMEM((3, 4, 64), BF16),
            pltpu.VMEM((6 * 64, 32), BF16),
            pltpu.VMEM((2 * 64, 256), BF16),
            pltpu.VMEM((2 * 64, 256), BF16),
            pltpu.VMEM((2, 16, 256), BF16),
            pltpu.VMEM((24, 64), F32),
            pltpu.VMEM((R, 14 * 64, 256), BF16),
            pltpu.VMEM((R, 12 * 64, 256), BF16),
            pltpu.VMEM((R, 10 * 64, 256), BF16),
            dma((8,)),
            dma((4,)),
            dma((2,)),
            dma((2,)),
            dma((2, G, NCH)),
            dma((SLABS, NCH)),
            dma((NCH,)),
            dma((NCH,)),
            dma((G, NCH)),
            dma((G, NCH)),
            pltpu.SemaphoreType.REGULAR,
        ],
        compiler_params=pltpu.CompilerParams(
            collective_id=0, has_side_effects=True, vmem_limit_bytes=32 * 1024 * 1024
        ),
        name="climate_step",
    )(*[pltpu.with_memory_space_constraint(v, pltpu.HBM) for v in arguments])
    return pl.pallas_call(
        second_kernel,
        out_shape=jax.ShapeDtypeStruct(fields.shape, F32),
        in_specs=[vmem],
        out_specs=anywhere,
        scratch_shapes=[pltpu.VMEM((32, 8, 256), F32), dma((4, 8))],
        compiler_params=pltpu.CompilerParams(vmem_limit_bytes=8 * 1024 * 1024),
        name="climate_end",
    )(updated)


def solution(mesh):
    return jax.shard_map(
        on_device,
        mesh=mesh,
        in_specs=(P(None, "wide", "lat", None), P(), P(), P(), P()),
        out_specs=P(None, "wide", "lat", None),
        check_vma=False,
    )
```

```python
import jax
import jax.numpy as jnp
from jax import lax
from jax.experimental import pallas as pl
from jax.experimental.pallas import tpu as pltpu
from jax.sharding import PartitionSpec as P

MESH = pl.DeviceIdType.MESH
F32 = jnp.float32
BF16 = jnp.bfloat16

G = 4
R = 9
STARTS = (0, 8, 17, 25)
CH = 3
NCH = R // CH
SLABS = G + 4
UPPER = ((0, 1, 2),)
LOWER = ((0, 1), (2,))


def face_terms(total):
    face = 0.075 * total
    square = face * face + 0.15 * 0.15 * 0.01
    return face, square * lax.rsqrt(square)


def spread(v, first):
    sub = lax.broadcasted_iota(jnp.int32, v.shape, 0)
    if first == 0:
        pair = jnp.where(sub < 2, v, pltpu.roll(v, 2, 0))
    else:
        pair = jnp.where(sub < 2, pltpu.roll(v, 6, 0), v)
    return jnp.where(sub < 4, pair, pltpu.roll(pair, 4, 0))


def transport(rows, masks):
    n = len(rows) - 2
    winds = [spread(v, 2) for v in rows]
    fluxes = []
    for j in range(n + 1):
        low, high = rows[j], rows[j + 1]
        face, speed = face_terms(winds[j] + winds[j + 1])
        flux = face * (low + high) - speed * (high - low)
        if j in masks:
            flux = flux * masks[j]
        fluxes.append(flux)
    outs = []
    for j in range(n):
        cell = rows[j + 1]
        lanes = cell.shape[1]
        wind = spread(cell, 0)
        face, speed = face_terms(wind + pltpu.roll(wind, lanes - 1, 1))
        after = pltpu.roll(cell, lanes - 1, 1)
        flux = face * (cell + after) - speed * (after - cell)
        div = flux - pltpu.roll(flux, 1, 1)
        outs.append(cell - (div + (fluxes[j + 1] - fluxes[j])))
    return outs


def act(t):
    return t + t * jnp.tanh(t)


def dot(a, b):
    return jnp.dot(a, b, preferred_element_type=F32)


def kernel(
    f_hbm, w1_hbm, w2_hbm, w3_hbm, w4_hbm, upd_ref,
    ext, adv, packed, xbuf, tsend, tin, w1_ref, w2_ref, w3_ref, w4_ref,
    band1, band2, band3, wd, stage, h1, h2, h3,
    in_sem, w_sem, halo_send, halo_recv, x_send, x_recv, f_send, f_recv, t_send, t_recv, ready,
):
    lat = lax.axis_index("lat")
    wide = lax.axis_index("wide")
    n_lat = lax.axis_size("lat")
    n_groups = lax.axis_size("wide") // G
    grp = wide // G
    m = wide % G
    at_south = lat == 0
    at_north = lat == n_lat - 1
    has_low = grp > 0
    has_high = grp < n_groups - 1
    cross_low = grp == n_groups // 2
    cross_high = grp == n_groups // 2 - 1
    up = m >= 2
    down = jnp.logical_and(has_low, jnp.logical_not(cross_low))
    has_other = jnp.logical_or(
        jnp.logical_and(up, has_high), jnp.logical_and(jnp.logical_not(up), down)
    )
    og = jnp.where(up, grp + 1, grp - 1)
    os = jnp.where(up, m - 2, m + G + 2)

    barrier = pltpu.get_barrier_semaphore()

    def greet(la, wi):
        pl.semaphore_signal(barrier, inc=1, device_id=(la, wi), device_id_type=MESH)

    @pl.when(has_low)
    def _():
        for k in (2, 3):
            greet(lat, (grp - 1) * G + k)

    @pl.when(jnp.logical_and(has_high, jnp.logical_not(cross_high)))
    def _():
        for k in (0, 1):
            greet(lat, (grp + 1) * G + k)

    @pl.when(jnp.logical_and(cross_low, jnp.logical_not(up)))
    def _():
        greet(lat, wide - G)

    for k in range(G):
        @pl.when(m != k)
        def _():
            greet(lat, grp * G + k)

    @pl.when(jnp.logical_not(at_south))
    def _():
        greet(lat - 1, wide)

    @pl.when(jnp.logical_not(at_north))
    def _():
        greet(lat + 1, wide)

    loads = []
    for f in range(4):
        for l in range(2):
            loads.append(
                pltpu.make_async_copy(
                    f_hbm.at[f, l], ext.at[pl.ds(2, 32), 2 * f + l], in_sem.at[2 * f + l]
                )
            )
    for c in loads:
        c.start()
    w_loads = [
        pltpu.make_async_copy(src, dst, w_sem.at[k])
        for k, (src, dst) in enumerate(
            ((w1_hbm, w1_ref), (w2_hbm, w2_ref), (w3_hbm, w3_ref), (w4_hbm, w4_ref))
        )
    ]
    for c in w_loads:
        c.start()

    @pl.when(at_south)
    def _():
        ext[0:2] = jnp.zeros((2, 8, 256), F32)

    @pl.when(at_north)
    def _():
        ext[34:36] = jnp.zeros((2, 8, 256), F32)

    @pl.when(grp == 0)
    def _():
        xbuf[0:2] = jnp.zeros((2, R, 8, 256), BF16)

    @pl.when(grp == n_groups - 1)
    def _():
        xbuf[G + 2 : G + 4] = jnp.zeros((2, R, 8, 256), BF16)

    for c in loads:
        c.wait()

    def local_row(k, c):
        return (NCH - 1 - c) * CH if k == 0 else c * CH

    def base_of(c):
        return jnp.where(m == 0, (NCH - 1 - c) * CH, c * CH)

    def first_transport(k, c, masks):
        e = STARTS[k] + local_row(k, c)
        n = CH - 1 if (k, c) == (2, NCH - 1) else CH
        outs = transport([ext[e + i] for i in range(n + 2)], masks)
        for i in range(n):
            adv[e + i] = outs[i]
            packed[e + i] = outs[i].astype(BF16)

    def x_copy(k, c, group, slab, other):
        row = local_row(k, c)
        return pltpu.make_async_remote_copy(
            packed.at[pl.ds(STARTS[k] + row, CH)],
            xbuf.at[slab, pl.ds(row, CH)],
            x_send.at[other, k, c],
            x_recv.at[slab, c],
            device_id=(lat, group * G + k),
            device_id_type=MESH,
        )

    def each_x(k, c, act_on):
        @pl.when(has_other)
        def _():
            act_on(x_copy(k, c, og, os, 1))

        @pl.when(m != k)
        def _():
            act_on(x_copy(k, c, grp, m + 2, 0))

    def send_x(k, c):
        each_x(k, c, lambda d: d.start())

    def x_arrived(slab, c):
        pltpu.make_async_remote_copy(
            packed.at[pl.ds(0, CH)], xbuf.at[slab, pl.ds(base_of(c), CH)],
            x_send.at[0, 0, c], x_recv.at[slab, c],
            device_id=(lat, wide), device_id_type=MESH,
        ).wait_recv()

    for k in range(G):
        first_transport(k, 0, {})

    expected = (
        (G - 1)
        + jnp.where(at_south, 0, 1)
        + jnp.where(at_north, 0, 1)
        + jnp.where(has_other, G, 0)
        + jnp.where(jnp.logical_and(cross_high, jnp.logical_not(up)), 1, 0)
    )
    pl.semaphore_wait(barrier, expected)

    @pl.when(cross_high)
    def _():
        pl.semaphore_signal(ready, inc=1, device_id=(lat, wide + G), device_id_type=MESH)

    to_north = pltpu.make_async_remote_copy(
        ext.at[pl.ds(32, 2)], ext.at[pl.ds(0, 2)], halo_send.at[0], halo_recv.at[0],
        device_id=(lat + 1, wide), device_id_type=MESH,
    )
    to_south = pltpu.make_async_remote_copy(
        ext.at[pl.ds(2, 2)], ext.at[pl.ds(34, 2)], halo_send.at[1], halo_recv.at[1],
        device_id=(lat - 1, wide), device_id_type=MESH,
    )

    @pl.when(jnp.logical_not(at_north))
    def _():
        to_north.start()

    @pl.when(jnp.logical_not(at_south))
    def _():
        to_south.start()

    for k in range(G):
        send_x(k, 0)
    for k in range(G):
        first_transport(k, 1, {})
    for k in range(G):
        send_x(k, 1)
    for k in (1, 2):
        first_transport(k, NCH - 1, {})
    for k in (1, 2):
        send_x(k, NCH - 1)

    for c in w_loads:
        c.wait()

    def iota(shape, d):
        return lax.broadcasted_iota(jnp.int32, shape, d)

    def one(cond):
        return jnp.where(cond, 1.0, 0.0)

    eye = one(iota((64, 64), 0) == iota((64, 64), 1)).astype(BF16)

    def transposed(w):
        return lax.dot_general(eye, w, (((1,), (1,)), ((), ())), preferred_element_type=F32)

    stage[...] = jnp.zeros((24, 64), F32)
    for k in range(3):
        stage[8 * k : 8 * k + 4] = w1_ref[k].astype(F32)
    w1t = (0.5 * transposed(stage[...].astype(BF16))).astype(BF16)

    row = iota((24, 32), 0)
    col = iota((24, 32), 1)
    same_field = (row & 7) == ((col & 7) >> 1)
    level_in = 2 * (col >> 3) + (col & 1)
    for j in range(6):
        tap = one(jnp.logical_and(same_field, level_in == j + (row >> 3))).astype(BF16)
        band1[64 * j : 64 * j + 64] = dot(w1t, tap).astype(BF16)
    zeros = jnp.zeros((64, 64), F32)
    for w_ref, band_ref in ((w2_ref, band2), (w3_ref, band3)):
        taps = [0.5 * transposed(w_ref[k]) for k in range(3)]
        for o in range(2):
            parts = [taps[i - o] if 0 <= i - o < 3 else zeros for i in range(4)]
            band_ref[64 * o : 64 * o + 64] = jnp.concatenate(parts, axis=1).astype(BF16)
    rho = iota((16, 64), 0)
    level_out = 2 * (rho >> 3) + (rho & 1)
    stage[0:8] = jnp.zeros((8, 64), F32)
    pick = one(iota((16, 8), 1) == ((iota((16, 8), 0) & 7) >> 1)).astype(BF16)
    last = []
    for k in range(3):
        stage[0:4] = w4_ref[k].astype(F32)
        last.append(dot(pick, stage[0:8].astype(BF16)))
    for t in range(2):
        parts = []
        for i in range(4):
            part = jnp.zeros((16, 64), F32)
            for k in range(3):
                part = part + jnp.where(level_out == 4 * t + i - k, last[k], 0.0)
            parts.append(part)
        wd[t] = jnp.concatenate(parts, axis=1).astype(BF16)

    @pl.when(jnp.logical_not(at_south))
    def _():
        to_north.wait_recv()

    @pl.when(jnp.logical_not(at_north))
    def _():
        to_south.wait_recv()

    first_transport(0, NCH - 1, {1: jnp.where(at_south, 0.0, 1.0).astype(F32)})
    first_transport(3, NCH - 1, {2: jnp.where(at_north, 0.0, 1.0).astype(F32)})
    for k in (0, 3):
        send_x(k, NCH - 1)

    def forward(c):
        return pltpu.make_async_remote_copy(
            xbuf.at[pl.ds(2, 2), pl.ds(base_of(c), CH)],
            xbuf.at[pl.ds(G + 2, 2), pl.ds(base_of(c), CH)],
            f_send.at[c],
            f_recv.at[c],
            device_id=(lat, wide - G),
            device_id_type=MESH,
        )

    low_valid = jnp.where(grp == 0, 0.0, 1.0).astype(F32)
    high_valid = jnp.where(grp == n_groups - 1, 0.0, 1.0).astype(F32)

    def t_copy(k, c):
        return pltpu.make_async_remote_copy(
            tsend.at[k, pl.ds(base_of(c), CH)],
            tin.at[m, pl.ds(base_of(c), CH)],
            t_send.at[k, c],
            t_recv.at[m, c],
            device_id=(lat, grp * G + k),
            device_id_type=MESH,
        )

    def store_act(dst, src, at, z, low, high):
        halves = ((0, 128, None),)
        if low is not None or high is not None:
            halves = ((0, 64, low), (64, 64, high))
        for o, size, valid in halves:
            part = z[o : o + size]
            if valid is not None:
                part = part * valid
            out = act(part)
            if src is not None:
                out = src[at + o + 64 : at + o + 64 + size].astype(F32) + out
            dst[at + o : at + o + size] = out.astype(BF16)

    def first_stage(row, slab, pairs, masks):
        r, at_row = row
        parts = [xbuf[s, r].astype(F32) for s in range(slab, slab + 4)]
        x = jnp.concatenate(parts, axis=0).astype(BF16)
        for p in pairs:
            at = 128 * (p - slab)
            z = dot(band1[at : at + 128], x)
            store_act(h1.at[at_row], None, 128 * p, z, *masks.get(p, (None, None)))

    def later_stage(dst, src, band, row, pairs, masks):
        for p in pairs:
            at = 128 * p
            z = dot(band[...], src[row[1], at : at + 256])
            store_act(dst.at[row[1]], src.at[row[1]], at, z, *masks.get(p, (None, None)))

    def finish(row, p, members):
        r, n_row = row
        at = 64 * p
        out = dot(wd[0], h3[n_row, at : at + 256]) + dot(wd[1][:, 0:128], h3[n_row, at + 256 : at + 384])
        for n, k in enumerate(members):
            tsend[k, r] = out[8 * n : 8 * n + 8].astype(BF16)

    def send_t(members, c):
        for k in members:
            @pl.when(m != k)
            def _():
                t_copy(k, c).start()

    def rows_of(chunks):
        return [(base_of(c) + i, CH * c + i) for c in chunks for i in range(CH)]

    mine = (25 * m + 1) // 3

    def relay(c):
        xbuf[pl.ds(m + 2, 1), pl.ds(base_of(c), CH)] = packed[pl.ds(mine + base_of(c), CH)][None]
        for k in range(G):
            @pl.when(m != k)
            def _():
                x_arrived(k + 2, c)

        @pl.when(cross_low)
        def _():
            if c == 0:
                pl.semaphore_wait(ready, 1)
            forward(c).start()

    def middle(chunks):
        rows = rows_of(chunks)
        for r in rows:
            first_stage(r, 2, (2, 3, 4), {})
        for r in rows:
            later_stage(h2, h1, band2, r, (2, 3), {})
        for r in rows:
            later_stage(h3, h2, band3, r, (2,), {})

    relay(0)
    relay(1)
    middle((0, 1))
    relay(2)
    middle((2,))

    def upper(chunks):
        for c in chunks:
            @pl.when(cross_high)
            def _():
                forward(c).wait_recv()

            @pl.when(jnp.logical_and(has_high, jnp.logical_not(cross_high)))
            def _():
                x_arrived(G + 2, c)
                x_arrived(G + 3, c)

        rows = rows_of(chunks)
        for r in rows:
            first_stage(r, 4, (5, 6), {5: (None, high_valid), 6: (high_valid, high_valid)})
        for r in rows:
            later_stage(h2, h1, band2, r, (4, 5), {5: (high_valid, high_valid)})
        for r in rows:
            later_stage(h3, h2, band3, r, (3, 4), {4: (None, high_valid)})
        for r in rows:
            finish(r, 4, (2, 3))
        for c in chunks:
            send_t((2, 3), c)

    def lower(chunks):
        for c in chunks:
            @pl.when(has_low)
            def _():
                x_arrived(0, c)
                x_arrived(1, c)

        rows = rows_of(chunks)
        for r in rows:
            first_stage(r, 0, (0, 1), {0: (low_valid, low_valid), 1: (low_valid, None)})
        for r in rows:
            later_stage(h2, h1, band2, r, (0, 1), {0: (low_valid, low_valid)})
        for r in rows:
            later_stage(h3, h2, band3, r, (0, 1), {0: (low_valid, None)})
        for r in rows:
            finish(r, 0, (0, 1))
        for c in chunks:
            send_t((0, 1), c)

    for chunks in UPPER:
        upper(chunks)
    for chunks in LOWER:
        lower(chunks)
    tin[pl.ds(m, 1)] = tsend[pl.ds(m, 1)]

    for k in range(G):
        @pl.when(m != k)
        def _():
            for c in range(NCH):
                pltpu.make_async_remote_copy(
                    tsend.at[k, pl.ds(local_row(k, c), CH)],
                    tin.at[k, pl.ds(local_row(k, c), CH)],
                    t_send.at[k, c], t_recv.at[k, c],
                    device_id=(lat, wide), device_id_type=MESH,
                ).wait_recv()

        first = STARTS[k] if k == 0 else STARTS[k - 1] + R
        for e in range(first, STARTS[k] + R):
            upd_ref[e] = adv[e] + tin[k, e - STARTS[k]].astype(F32)

    @pl.when(jnp.logical_not(at_north))
    def _():
        to_north.wait_send()

    @pl.when(jnp.logical_not(at_south))
    def _():
        to_south.wait_send()

    for c in range(NCH):
        @pl.when(cross_low)
        def _():
            forward(c).wait_send()

        for k in range(G):
            each_x(k, c, lambda d: d.wait_send())

            @pl.when(m != k)
            def _():
                t_copy(k, c).wait_send()


def second_kernel(upd_ref, out_ref, outv, sem):
    lat = lax.axis_index("lat")
    at_south = lat == 0
    at_north = lat == lax.axis_size("lat") - 1
    stores = []
    for c in range(4):
        masks = {}
        if c == 0:
            masks = {0: jnp.where(at_south, 0.0, 1.0).astype(F32)}
        if c == 3:
            masks = {8: jnp.where(at_north, 0.0, 1.0).astype(F32)}
        e = 8 * c
        outs = transport([upd_ref[e + i] for i in range(10)], masks)
        for i in range(8):
            outv[e + i] = outs[i]
        for f in range(4):
            for l in range(2):
                d = pltpu.make_async_copy(
                    outv.at[pl.ds(e, 8), 2 * f + l],
                    out_ref.at[f, l, pl.ds(e, 8)],
                    sem.at[c, 2 * f + l],
                )
                d.start()
                stores.append(d)
    for d in stores:
        d.wait()


def on_device(fields, w_first, w_second, w_third, w_last):
    anywhere = pl.BlockSpec(memory_space=pltpu.HBM)
    vmem = pl.BlockSpec(memory_space=pltpu.VMEM)
    dma = pltpu.SemaphoreType.DMA
    arguments = (fields, w_first, w_second, w_third, jnp.transpose(w_last, (0, 2, 1)))
    updated = pl.pallas_call(
        kernel,
        out_shape=jax.ShapeDtypeStruct((34, 8, 256), F32),
        in_specs=[anywhere] * 5,
        out_specs=vmem,
        scratch_shapes=[
            pltpu.VMEM((36, 8, 256), F32),
            pltpu.VMEM((34, 8, 256), F32),
            pltpu.VMEM((34, 8, 256), BF16),
            pltpu.VMEM((SLABS, R, 8, 256), BF16),
            pltpu.VMEM((G, R, 8, 256), BF16),
            pltpu.VMEM((G, R, 8, 256), BF16),
            pltpu.VMEM((3, 4, 64), BF16),
            pltpu.VMEM((3, 64, 64), BF16),
            pltpu.VMEM((3, 64, 64), BF16),
            pltpu.VMEM((3, 4, 64), BF16),
            pltpu.VMEM((6 * 64, 32), BF16),
            pltpu.VMEM((2 * 64, 256), BF16),
            pltpu.VMEM((2 * 64, 256), BF16),
            pltpu.VMEM((2, 16, 256), BF16),
            pltpu.VMEM((24, 64), F32),
            pltpu.VMEM((R, 14 * 64, 256), BF16),
            pltpu.VMEM((R, 12 * 64, 256), BF16),
            pltpu.VMEM((R, 10 * 64, 256), BF16),
            dma((8,)),
            dma((4,)),
            dma((2,)),
            dma((2,)),
            dma((2, G, NCH)),
            dma((SLABS, NCH)),
            dma((NCH,)),
            dma((NCH,)),
            dma((G, NCH)),
            dma((G, NCH)),
            pltpu.SemaphoreType.REGULAR,
        ],
        compiler_params=pltpu.CompilerParams(
            collective_id=0, has_side_effects=True, vmem_limit_bytes=32 * 1024 * 1024
        ),
        name="climate_step",
    )(*[pltpu.with_memory_space_constraint(v, pltpu.HBM) for v in arguments])
    return pl.pallas_call(
        second_kernel,
        out_shape=jax.ShapeDtypeStruct(fields.shape, F32),
        in_specs=[vmem],
        out_specs=anywhere,
        scratch_shapes=[pltpu.VMEM((32, 8, 256), F32), dma((4, 8))],
        compiler_params=pltpu.CompilerParams(vmem_limit_bytes=8 * 1024 * 1024),
        name="climate_end",
    )(updated)


def solution(mesh):
    return jax.shard_map(
        on_device,
        mesh=mesh,
        in_specs=(P(None, "wide", "lat", None), P(), P(), P(), P()),
        out_specs=P(None, "wide", "lat", None),
        check_vma=False,
    )
```

```python
import jax
import jax.numpy as jnp
from jax import lax
from jax.experimental import pallas as pl
from jax.experimental.pallas import tpu as pltpu
from jax.sharding import PartitionSpec as P

MESH = pl.DeviceIdType.MESH
F32 = jnp.float32
BF16 = jnp.bfloat16

G = 4
R = 9
STARTS = (0, 8, 17, 25)
CH = 3
NCH = R // CH
SLABS = G + 4
UPPER = ((0, 1, 2),)
LOWER = ((0, 1), (2,))


def face_terms(total):
    face = 0.075 * total
    square = face * face + 0.15 * 0.15 * 0.01
    return face, square * lax.rsqrt(square)


def spread(v, first):
    sub = lax.broadcasted_iota(jnp.int32, v.shape, 0)
    if first == 0:
        pair = jnp.where(sub < 2, v, pltpu.roll(v, 2, 0))
    else:
        pair = jnp.where(sub < 2, pltpu.roll(v, 6, 0), v)
    return jnp.where(sub < 4, pair, pltpu.roll(pair, 4, 0))


def transport(rows, masks):
    n = len(rows) - 2
    winds = [spread(v, 2) for v in rows]
    fluxes = []
    for j in range(n + 1):
        low, high = rows[j], rows[j + 1]
        face, speed = face_terms(winds[j] + winds[j + 1])
        flux = face * (low + high) - speed * (high - low)
        if j in masks:
            flux = flux * masks[j]
        fluxes.append(flux)
    outs = []
    for j in range(n):
        cell = rows[j + 1]
        lanes = cell.shape[1]
        wind = spread(cell, 0)
        face, speed = face_terms(wind + pltpu.roll(wind, lanes - 1, 1))
        after = pltpu.roll(cell, lanes - 1, 1)
        flux = face * (cell + after) - speed * (after - cell)
        div = flux - pltpu.roll(flux, 1, 1)
        outs.append(cell - (div + (fluxes[j + 1] - fluxes[j])))
    return outs


def act(t):
    return t + t * jnp.tanh(t)


def dot(a, b):
    return jnp.dot(a, b, preferred_element_type=F32)


def kernel(
    f_hbm, w1_hbm, w2_hbm, w3_hbm, w4_hbm, upd_ref,
    ext, adv, packed, xbuf, tsend, tin, w1_ref, w2_ref, w3_ref, w4_ref,
    band1, band2, band3, wd, stage, h1, h2, h3,
    in_sem, w_sem, halo_send, halo_recv, x_send, x_recv, f_send, f_recv, t_send, t_recv, ready,
):
    lat = lax.axis_index("lat")
    wide = lax.axis_index("wide")
    n_lat = lax.axis_size("lat")
    n_groups = lax.axis_size("wide") // G
    grp = wide // G
    m = wide % G
    at_south = lat == 0
    at_north = lat == n_lat - 1
    has_low = grp > 0
    has_high = grp < n_groups - 1
    cross_low = grp == n_groups // 2
    cross_high = grp == n_groups // 2 - 1
    up = m >= 2
    down = jnp.logical_and(has_low, jnp.logical_not(cross_low))
    has_other = jnp.logical_or(
        jnp.logical_and(up, has_high), jnp.logical_and(jnp.logical_not(up), down)
    )
    og = jnp.where(up, grp + 1, grp - 1)
    os = jnp.where(up, m - 2, m + G + 2)

    barrier = pltpu.get_barrier_semaphore()

    def greet(la, wi):
        pl.semaphore_signal(barrier, inc=1, device_id=(la, wi), device_id_type=MESH)

    @pl.when(has_low)
    def _():
        for k in (2, 3):
            greet(lat, (grp - 1) * G + k)

    @pl.when(jnp.logical_and(has_high, jnp.logical_not(cross_high)))
    def _():
        for k in (0, 1):
            greet(lat, (grp + 1) * G + k)

    @pl.when(jnp.logical_and(cross_low, jnp.logical_not(up)))
    def _():
        greet(lat, wide - G)

    for k in range(G):
        @pl.when(m != k)
        def _():
            greet(lat, grp * G + k)

    @pl.when(jnp.logical_not(at_south))
    def _():
        greet(lat - 1, wide)

    @pl.when(jnp.logical_not(at_north))
    def _():
        greet(lat + 1, wide)

    loads = []
    for f in range(4):
        for l in range(2):
            loads.append(
                pltpu.make_async_copy(
                    f_hbm.at[f, l], ext.at[pl.ds(2, 32), 2 * f + l], in_sem.at[2 * f + l]
                )
            )
    for c in loads:
        c.start()
    w_loads = [
        pltpu.make_async_copy(src, dst, w_sem.at[k])
        for k, (src, dst) in enumerate(
            ((w1_hbm, w1_ref), (w2_hbm, w2_ref), (w3_hbm, w3_ref), (w4_hbm, w4_ref))
        )
    ]
    for c in w_loads:
        c.start()

    @pl.when(at_south)
    def _():
        ext[0:2] = jnp.zeros((2, 8, 256), F32)

    @pl.when(at_north)
    def _():
        ext[34:36] = jnp.zeros((2, 8, 256), F32)

    @pl.when(grp == 0)
    def _():
        xbuf[0:2] = jnp.zeros((2, R, 8, 256), BF16)

    @pl.when(grp == n_groups - 1)
    def _():
        xbuf[G + 2 : G + 4] = jnp.zeros((2, R, 8, 256), BF16)

    for c in loads:
        c.wait()

    def local_row(k, c):
        return (NCH - 1 - c) * CH if k == 0 else c * CH

    def base_of(c):
        return jnp.where(m == 0, (NCH - 1 - c) * CH, c * CH)

    def first_transport(k, c, masks):
        e = STARTS[k] + local_row(k, c)
        n = CH - 1 if (k, c) == (2, NCH - 1) else CH
        outs = transport([ext[e + i] for i in range(n + 2)], masks)
        for i in range(n):
            adv[e + i] = outs[i]
            packed[e + i] = outs[i].astype(BF16)

    def x_copy(k, c, group, slab, other):
        row = local_row(k, c)
        return pltpu.make_async_remote_copy(
            packed.at[pl.ds(STARTS[k] + row, CH)],
            xbuf.at[slab, pl.ds(row, CH)],
            x_send.at[other, k, c],
            x_recv.at[slab, c],
            device_id=(lat, group * G + k),
            device_id_type=MESH,
        )

    def each_x(k, c, act_on):
        @pl.when(has_other)
        def _():
            act_on(x_copy(k, c, og, os, 1))

        @pl.when(m != k)
        def _():
            act_on(x_copy(k, c, grp, m + 2, 0))

    def send_x(k, c):
        each_x(k, c, lambda d: d.start())

    def x_arrived(slab, c):
        pltpu.make_async_remote_copy(
            packed.at[pl.ds(0, CH)], xbuf.at[slab, pl.ds(base_of(c), CH)],
            x_send.at[0, 0, c], x_recv.at[slab, c],
            device_id=(lat, wide), device_id_type=MESH,
        ).wait_recv()

    for k in range(G):
        first_transport(k, 0, {})

    expected = (
        (G - 1)
        + jnp.where(at_south, 0, 1)
        + jnp.where(at_north, 0, 1)
        + jnp.where(has_other, G, 0)
        + jnp.where(jnp.logical_and(cross_high, jnp.logical_not(up)), 1, 0)
    )
    pl.semaphore_wait(barrier, expected)

    @pl.when(cross_high)
    def _():
        pl.semaphore_signal(ready, inc=1, device_id=(lat, wide + G), device_id_type=MESH)

    to_north = pltpu.make_async_remote_copy(
        ext.at[pl.ds(32, 2)], ext.at[pl.ds(0, 2)], halo_send.at[0], halo_recv.at[0],
        device_id=(lat + 1, wide), device_id_type=MESH,
    )
    to_south = pltpu.make_async_remote_copy(
        ext.at[pl.ds(2, 2)], ext.at[pl.ds(34, 2)], halo_send.at[1], halo_recv.at[1],
        device_id=(lat - 1, wide), device_id_type=MESH,
    )

    @pl.when(jnp.logical_not(at_north))
    def _():
        to_north.start()

    @pl.when(jnp.logical_not(at_south))
    def _():
        to_south.start()

    for k in range(G):
        send_x(k, 0)
    for k in range(G):
        first_transport(k, 1, {})
    for k in range(G):
        send_x(k, 1)
    for k in (1, 2):
        first_transport(k, NCH - 1, {})
    for k in (1, 2):
        send_x(k, NCH - 1)

    for c in w_loads:
        c.wait()

    def iota(shape, d):
        return lax.broadcasted_iota(jnp.int32, shape, d)

    def one(cond):
        return jnp.where(cond, 1.0, 0.0)

    eye = one(iota((64, 64), 0) == iota((64, 64), 1)).astype(BF16)

    def transposed(w):
        return lax.dot_general(eye, w, (((1,), (1,)), ((), ())), preferred_element_type=F32)

    stage[...] = jnp.zeros((24, 64), F32)
    for k in range(3):
        stage[8 * k : 8 * k + 4] = w1_ref[k].astype(F32)
    w1t = (0.5 * transposed(stage[...].astype(BF16))).astype(BF16)

    row = iota((24, 32), 0)
    col = iota((24, 32), 1)
    same_field = (row & 7) == ((col & 7) >> 1)
    level_in = 2 * (col >> 3) + (col & 1)
    for j in range(6):
        tap = one(jnp.logical_and(same_field, level_in == j + (row >> 3))).astype(BF16)
        band1[64 * j : 64 * j + 64] = dot(w1t, tap).astype(BF16)
    zeros = jnp.zeros((64, 64), F32)
    for w_ref, band_ref in ((w2_ref, band2), (w3_ref, band3)):
        taps = [0.5 * transposed(w_ref[k]) for k in range(3)]
        for o in range(2):
            parts = [taps[i - o] if 0 <= i - o < 3 else zeros for i in range(4)]
            band_ref[64 * o : 64 * o + 64] = jnp.concatenate(parts, axis=1).astype(BF16)
    rho = iota((16, 64), 0)
    level_out = 2 * (rho >> 3) + (rho & 1)
    stage[0:8] = jnp.zeros((8, 64), F32)
    pick = one(iota((16, 8), 1) == ((iota((16, 8), 0) & 7) >> 1)).astype(BF16)
    last = []
    for k in range(3):
        stage[0:4] = w4_ref[k].astype(F32)
        last.append(dot(pick, stage[0:8].astype(BF16)))
    for t in range(2):
        parts = []
        for i in range(4):
            part = jnp.zeros((16, 64), F32)
            for k in range(3):
                part = part + jnp.where(level_out == 4 * t + i - k, last[k], 0.0)
            parts.append(part)
        wd[t] = jnp.concatenate(parts, axis=1).astype(BF16)

    @pl.when(jnp.logical_not(at_south))
    def _():
        to_north.wait_recv()

    @pl.when(jnp.logical_not(at_north))
    def _():
        to_south.wait_recv()

    first_transport(0, NCH - 1, {1: jnp.where(at_south, 0.0, 1.0).astype(F32)})
    first_transport(3, NCH - 1, {2: jnp.where(at_north, 0.0, 1.0).astype(F32)})
    for k in (0, 3):
        send_x(k, NCH - 1)

    def forward(c):
        return pltpu.make_async_remote_copy(
            xbuf.at[pl.ds(2, 2), pl.ds(base_of(c), CH)],
            xbuf.at[pl.ds(G + 2, 2), pl.ds(base_of(c), CH)],
            f_send.at[c],
            f_recv.at[c],
            device_id=(lat, wide - G),
            device_id_type=MESH,
        )

    low_valid = jnp.where(grp == 0, 0.0, 1.0).astype(F32)
    high_valid = jnp.where(grp == n_groups - 1, 0.0, 1.0).astype(F32)

    def t_copy(k, c):
        return pltpu.make_async_remote_copy(
            tsend.at[k, pl.ds(base_of(c), CH)],
            tin.at[m, pl.ds(base_of(c), CH)],
            t_send.at[k, c],
            t_recv.at[m, c],
            device_id=(lat, grp * G + k),
            device_id_type=MESH,
        )

    def store_act(dst, src, at, z, low, high):
        halves = ((0, 128, None),)
        if low is not None or high is not None:
            halves = ((0, 64, low), (64, 64, high))
        for o, size, valid in halves:
            part = z[o : o + size]
            if valid is not None:
                part = part * valid
            out = act(part)
            if src is not None:
                out = src[at + o + 64 : at + o + 64 + size].astype(F32) + out
            dst[at + o : at + o + size] = out.astype(BF16)

    def first_stage(row, slab, pairs, masks):
        r, at_row = row
        parts = [xbuf[s, r].astype(F32) for s in range(slab, slab + 4)]
        x = jnp.concatenate(parts, axis=0).astype(BF16)
        for p in pairs:
            at = 128 * (p - slab)
            z = dot(band1[at : at + 128], x)
            store_act(h1.at[at_row], None, 128 * p, z, *masks.get(p, (None, None)))

    def later_stage(dst, src, band, row, pairs, masks):
        for p in pairs:
            at = 128 * p
            z = dot(band[...], src[row[1], at : at + 256])
            store_act(dst.at[row[1]], src.at[row[1]], at, z, *masks.get(p, (None, None)))

    def finish(row, p, members):
        r, n_row = row
        at = 64 * p
        out = dot(wd[0], h3[n_row, at : at + 256]) + dot(wd[1][:, 0:128], h3[n_row, at + 256 : at + 384])
        for n, k in enumerate(members):
            tsend[k, r] = out[8 * n : 8 * n + 8].astype(BF16)

    def send_t(members, c):
        for k in members:
            @pl.when(m != k)
            def _():
                t_copy(k, c).start()

    def rows_of(chunks):
        return [(base_of(c) + i, CH * c + i) for c in chunks for i in range(CH)]

    mine = (25 * m + 1) // 3

    def relay(c):
        xbuf[pl.ds(m + 2, 1), pl.ds(base_of(c), CH)] = packed[pl.ds(mine + base_of(c), CH)][None]
        for k in range(G):
            @pl.when(m != k)
            def _():
                x_arrived(k + 2, c)

        @pl.when(cross_low)
        def _():
            if c == 0:
                pl.semaphore_wait(ready, 1)
            forward(c).start()

    def middle(chunks):
        rows = rows_of(chunks)
        for r in rows:
            first_stage(r, 2, (2, 3, 4), {})
        for r in rows:
            later_stage(h2, h1, band2, r, (2, 3), {})
        for r in rows:
            later_stage(h3, h2, band3, r, (2,), {})

    relay(0)
    relay(1)
    middle((0, 1))
    relay(2)
    middle((2,))

    def upper(chunks):
        for c in chunks:
            @pl.when(cross_high)
            def _():
                forward(c).wait_recv()

            @pl.when(jnp.logical_and(has_high, jnp.logical_not(cross_high)))
            def _():
                x_arrived(G + 2, c)
                x_arrived(G + 3, c)

        rows = rows_of(chunks)
        for r in rows:
            first_stage(r, 4, (5, 6), {5: (None, high_valid), 6: (high_valid, high_valid)})
        for r in rows:
            later_stage(h2, h1, band2, r, (4, 5), {5: (high_valid, high_valid)})
        for r in rows:
            later_stage(h3, h2, band3, r, (3, 4), {4: (None, high_valid)})
        for r in rows:
            finish(r, 4, (2, 3))
        for c in chunks:
            send_t((2, 3), c)

    def lower(chunks):
        for c in chunks:
            @pl.when(has_low)
            def _():
                x_arrived(0, c)
                x_arrived(1, c)

        rows = rows_of(chunks)
        for r in rows:
            first_stage(r, 0, (0, 1), {0: (low_valid, low_valid), 1: (low_valid, None)})
        for r in rows:
            later_stage(h2, h1, band2, r, (0, 1), {0: (low_valid, low_valid)})
        for r in rows:
            later_stage(h3, h2, band3, r, (0, 1), {0: (low_valid, None)})
        for r in rows:
            finish(r, 0, (0, 1))
        for c in chunks:
            send_t((0, 1), c)

    for chunks in UPPER:
        upper(chunks)
    for chunks in LOWER:
        lower(chunks)
    tin[pl.ds(m, 1)] = tsend[pl.ds(m, 1)]

    @pl.when(jnp.logical_not(at_north))
    def _():
        to_north.wait_send()

    @pl.when(jnp.logical_not(at_south))
    def _():
        to_south.wait_send()

    for c in range(NCH):
        @pl.when(cross_low)
        def _():
            forward(c).wait_send()

        for k in range(G):
            each_x(k, c, lambda d: d.wait_send())

            @pl.when(m != k)
            def _():
                t_copy(k, c).wait_send()

    for k in range(G):
        @pl.when(m != k)
        def _():
            for c in range(NCH):
                pltpu.make_async_remote_copy(
                    tsend.at[k, pl.ds(local_row(k, c), CH)],
                    tin.at[k, pl.ds(local_row(k, c), CH)],
                    t_send.at[k, c], t_recv.at[k, c],
                    device_id=(lat, wide), device_id_type=MESH,
                ).wait_recv()

        first = STARTS[k] if k == 0 else STARTS[k - 1] + R
        for e in range(first, STARTS[k] + R):
            upd_ref[e] = adv[e] + tin[k, e - STARTS[k]].astype(F32)


def second_kernel(upd_ref, out_ref, outv, sem):
    lat = lax.axis_index("lat")
    at_south = lat == 0
    at_north = lat == lax.axis_size("lat") - 1
    stores = []
    for c in range(4):
        masks = {}
        if c == 0:
            masks = {0: jnp.where(at_south, 0.0, 1.0).astype(F32)}
        if c == 3:
            masks = {8: jnp.where(at_north, 0.0, 1.0).astype(F32)}
        e = 8 * c
        outs = transport([upd_ref[e + i] for i in range(10)], masks)
        for i in range(8):
            outv[e + i] = outs[i]
        for f in range(4):
            for l in range(2):
                d = pltpu.make_async_copy(
                    outv.at[pl.ds(e, 8), 2 * f + l],
                    out_ref.at[f, l, pl.ds(e, 8)],
                    sem.at[c, 2 * f + l],
                )
                d.start()
                stores.append(d)
    for d in stores:
        d.wait()


def on_device(fields, w_first, w_second, w_third, w_last):
    anywhere = pl.BlockSpec(memory_space=pltpu.HBM)
    vmem = pl.BlockSpec(memory_space=pltpu.VMEM)
    dma = pltpu.SemaphoreType.DMA
    arguments = (fields, w_first, w_second, w_third, jnp.transpose(w_last, (0, 2, 1)))
    updated = pl.pallas_call(
        kernel,
        out_shape=jax.ShapeDtypeStruct((34, 8, 256), F32),
        in_specs=[anywhere] * 5,
        out_specs=vmem,
        scratch_shapes=[
            pltpu.VMEM((36, 8, 256), F32),
            pltpu.VMEM((34, 8, 256), F32),
            pltpu.VMEM((34, 8, 256), BF16),
            pltpu.VMEM((SLABS, R, 8, 256), BF16),
            pltpu.VMEM((G, R, 8, 256), BF16),
            pltpu.VMEM((G, R, 8, 256), BF16),
            pltpu.VMEM((3, 4, 64), BF16),
            pltpu.VMEM((3, 64, 64), BF16),
            pltpu.VMEM((3, 64, 64), BF16),
            pltpu.VMEM((3, 4, 64), BF16),
            pltpu.VMEM((6 * 64, 32), BF16),
            pltpu.VMEM((2 * 64, 256), BF16),
            pltpu.VMEM((2 * 64, 256), BF16),
            pltpu.VMEM((2, 16, 256), BF16),
            pltpu.VMEM((24, 64), F32),
            pltpu.VMEM((R, 14 * 64, 256), BF16),
            pltpu.VMEM((R, 12 * 64, 256), BF16),
            pltpu.VMEM((R, 10 * 64, 256), BF16),
            dma((8,)),
            dma((4,)),
            dma((2,)),
            dma((2,)),
            dma((2, G, NCH)),
            dma((SLABS, NCH)),
            dma((NCH,)),
            dma((NCH,)),
            dma((G, NCH)),
            dma((G, NCH)),
            pltpu.SemaphoreType.REGULAR,
        ],
        compiler_params=pltpu.CompilerParams(
            collective_id=0, has_side_effects=True, vmem_limit_bytes=32 * 1024 * 1024
        ),
        name="climate_step",
    )(*[pltpu.with_memory_space_constraint(v, pltpu.HBM) for v in arguments])
    return pl.pallas_call(
        second_kernel,
        out_shape=jax.ShapeDtypeStruct(fields.shape, F32),
        in_specs=[vmem],
        out_specs=anywhere,
        scratch_shapes=[pltpu.VMEM((32, 8, 256), F32), dma((4, 8))],
        compiler_params=pltpu.CompilerParams(vmem_limit_bytes=8 * 1024 * 1024),
        name="climate_end",
    )(updated)


def solution(mesh):
    return jax.shard_map(
        on_device,
        mesh=mesh,
        in_specs=(P(None, "wide", "lat", None), P(), P(), P(), P()),
        out_specs=P(None, "wide", "lat", None),
        check_vma=False,
    )
```
